128 devices in a mesh: sta: 8 (over x, y_hi), gx: 4 (over z), gy: 4 (over y_lo, core).
Axes of the slice: x: 4, y: 4 (y_hi: 2, y_lo: 2; y = y_hi * 2 + y_lo), z: 4, core: 2. Of those that a mesh axis runs over, the one named last changes fastest.
Arguments:
- rec_state: float32 [8, 4, 9, 32, 32, 128], P('sta', None, None, 'gx', 'gy'), may hold values from -6 to 6
- source_strain: bfloat16 [8, 8, 6, 32, 32, 128], P('sta', None, None, 'gx', 'gy'), may hold values from -6 to 6
- material: int32 [32, 32, 128], P('gx', 'gy'), may hold values from 0 to 15
- material_table: float32 [16, 3], replicated, may hold values from 0.5 to 1.5
- residual: float32 [8, 4, 8], P('sta'), may hold values from -4 to 4
- rec_cell: int32 [8, 4], P('sta'), may hold values from 0 to 1023
- listed: int32 [2, 8, 8], replicated, may hold values 0 or 1
- src_pick: int32 [2, 8], replicated, may hold values from 0 to 7
Outputs:
- kernels: float32 [2, 32, 32, 128], P(None, ('gx', 'sta'), 'gy')
The draws below stay inside these ranges and needn't reach their ends.
All inputs are finite; a program needn't handle non-finite values.
Results may differ from the reference program's by a relative error of at most 0.0003.
Values may be sent and summed in bfloat16 or wider, within the bound.
A program may use at most 128 MiB of HBM per device.

```python
import jax
import jax.numpy as jnp
from jax import lax

CZ = 128
REC = 4
STEPS = 8
TURNS = 2
NMAT = 16
NX = 32
NY = 32
N_STA = 8


def place_ends(result, stream_key, least, high):
    longest = result.shape.index(max(result.shape))
    spots = []
    for shift in (0, 1):
        where = [jax.random.randint(jax.random.fold_in(stream_key, axis), (), 0, length) for axis, length in enumerate(result.shape)]
        where[longest] = (where[longest] + shift) % result.shape[longest]
        spots.append(tuple(where))
    return result.at[spots[0]].set(least).at[spots[1]].set(high)


def steps_of(stream_key, dims, cuts, low, high):
    gain, own = 1.0, jax.random.fold_in(stream_key, 6)
    for axis_at, parts in cuts:
        draws = jnp.exp(jax.random.uniform(jax.random.fold_in(own, axis_at), (parts,), jnp.float32, low / len(cuts), high / len(cuts)))
        gain = gain * jnp.repeat(draws, dims[axis_at] // parts).reshape([-1 if axis == axis_at else 1 for axis in range(len(dims))])
    return gain


def noise(key, extent, deviation, most, split=(), kind=jnp.bfloat16):
    loudness = steps_of(key, extent, split, -0.22, 0.18) if split else 1.0
    result = jax.random.normal(key, extent, jnp.float32) * deviation * loudness
    return jnp.minimum(jnp.maximum(result, -most), most).astype(kind)


def setup_inputs(seed: int = 0) -> dict:
    streams_of = jax.random.split(jax.random.key(seed), 9)
    rec_state = noise(streams_of[0], (N_STA, REC, 9, NX, NY, CZ), 1.0, 6.0, ((0, 8), (3, 4), (4, 4)), jnp.float32)
    source_strain = noise(streams_of[1], (N_STA, STEPS, 6, NX, NY, CZ), 1.0, 6.0, ((0, 8), (3, 4), (4, 4)))
    material = place_ends(jax.random.randint(streams_of[2], (NX, NY, CZ), 0, NMAT), jax.random.fold_in(streams_of[2], 1), 0, NMAT - 1).astype(jnp.int32)
    material_table = jnp.clip(jax.random.uniform(streams_of[3], (NMAT, 3), jnp.float32, 0.5, 1.5), 0.5, 1.5)
    residual = noise(streams_of[4], (N_STA, REC, STEPS), 1.0, 4.0, ((0, 8),), jnp.float32)
    rec_cell = place_ends(jax.random.randint(streams_of[5], (N_STA, REC), 0, NX * NY), jax.random.fold_in(streams_of[5], 1), 0, (NX * NY) - 1).astype(jnp.int32)
    listed = place_ends((jax.random.randint(streams_of[6], (TURNS, STEPS, N_STA), 0, 2) < 1).astype(jnp.int32), jax.random.fold_in(streams_of[6], 1), 0, 1)
    src_pick = place_ends(jax.random.randint(streams_of[7], (TURNS, STEPS), 0, N_STA), jax.random.fold_in(streams_of[7], 1), 0, N_STA - 1).astype(jnp.int32)
    return {"rec_state": rec_state, "source_strain": source_strain, "material": material, "material_table": material_table, "residual": residual, "rec_cell": rec_cell, "listed": listed, "src_pick": src_pick}


C_NEAR = 8.0 / 12.0
C_FAR = -1.0 / 12.0
TIME_STEP = 0.25
AMPLITUDE = 4.0
KERNEL_SCALE = 0.0625
STIFFNESS = 0.3


def along_first(padded):
    core = padded[..., :, 2:-2, 2:-2]
    return C_NEAR * (core[..., 3:-1, :, :] - core[..., 1:-3, :, :]) + C_FAR * (core[..., 4:, :, :] - core[..., :-4, :, :])


def along_second(padded):
    core = padded[..., 2:-2, :, 2:-2]
    return C_NEAR * (core[..., :, 3:-1, :] - core[..., :, 1:-3, :]) + C_FAR * (core[..., :, 4:, :] - core[..., :, :-4, :])


def along_depth(padded):
    core = padded[..., 2:-2, 2:-2, :]
    return C_NEAR * (core[..., 3:-1] - core[..., 1:-3]) + C_FAR * (core[..., 4:] - core[..., :-4])


def pad_all(field):
    return jnp.pad(field, [(0, 0)] * (field.ndim - 3) + [(2, 2)] * 3)


def force_terms(padded, source_term):
    first = along_first(padded[:, 0]) + along_second(padded[:, 3]) + along_depth(padded[:, 4])
    second = along_first(padded[:, 3]) + along_second(padded[:, 1]) + along_depth(padded[:, 5])
    third = along_first(padded[:, 4]) + along_second(padded[:, 5]) + along_depth(padded[:, 2]) + source_term
    return jnp.stack([first, second, third], 1)


def strain_rates(padded):
    comp_first = padded[:, 0]
    comp_second = padded[:, 1]
    comp_depth = padded[:, 2]
    rate_first = along_first(comp_first)
    rate_second = along_second(comp_second)
    rate_depth = along_depth(comp_depth)
    shear_plane = 0.5 * (along_second(comp_first) + along_first(comp_second))
    shear_first = 0.5 * (along_depth(comp_first) + along_first(comp_depth))
    shear_second = 0.5 * (along_depth(comp_second) + along_second(comp_depth))
    return jnp.stack([rate_first, rate_second, rate_depth, shear_plane, shear_first, shear_second], 1)


def update_stress(stress, rates, lame, shear):
    trace = rates[:, 0] + rates[:, 1] + rates[:, 2]
    diagonal = stress[:, :3] + TIME_STEP * (lame * trace[:, None] + 2.0 * shear * rates[:, :3])
    offdiag = stress[:, 3:] + TIME_STEP * (2.0 * shear * rates[:, 3:])
    return jnp.concatenate([diagonal, offdiag], 1)


def correlate(source, weighted):
    trace_src = source[0] + source[1] + source[2]
    trace_rec = weighted[0] + weighted[1] + weighted[2]
    lam_part = trace_src * trace_rec
    diag_part = source[0] * weighted[0] + source[1] * weighted[1] + source[2] * weighted[2]
    off_part = source[3] * weighted[3] + source[4] * weighted[4] + source[5] * weighted[5]
    return jnp.stack([lam_part, 2.0 * diag_part + 4.0 * off_part])


def reference(rec_state, source_strain, material, material_table, residual, rec_cell, listed, src_pick):
    buoyancy = TIME_STEP / material_table[:, 0][material]
    lame = STIFFNESS * material_table[:, 1][material]
    shear = STIFFNESS * material_table[:, 2][material]
    depth_first = (jnp.arange(CZ) == 0).astype(jnp.float32)
    moments = jnp.arange(STEPS, dtype=jnp.int32)
    picked = source_strain[src_pick, moments[None, :]].astype(jnp.float32)
    row_index = jnp.arange(NX, dtype=jnp.int32)
    col_index = jnp.arange(NY, dtype=jnp.int32)

    def one_group(kernel, group):
        state = lax.dynamic_index_in_dim(rec_state, group, 0, keepdims=False)
        weights = lax.dynamic_index_in_dim(listed, group, 2, keepdims=False).astype(jnp.float32)
        cells = lax.dynamic_index_in_dim(rec_cell, group, 0, keepdims=False)
        res_rows = lax.dynamic_index_in_dim(residual, group, 0, keepdims=False)
        spots = ((cells // NY)[:, None, None] == row_index[None, :, None]) & ((cells % NY)[:, None, None] == col_index[None, None, :])
        spots = spots.astype(jnp.float32)
        velocity = state[:, :3]
        stress = state[:, 3:]
        for moment in range(STEPS):
            source_term = (AMPLITUDE * res_rows[:, moment])[:, None, None, None] * spots[:, :, :, None] * depth_first
            velocity = velocity + buoyancy * force_terms(pad_all(stress), source_term)
            rates = strain_rates(pad_all(velocity))
            stress = update_stress(stress, rates, lame, shear)
            weighted = jnp.sum((KERNEL_SCALE * res_rows[:, moment])[:, None, None, None, None] * rates, 0)
            combined = jnp.sum(weights[:, moment][:, None, None, None, None] * picked[:, moment], 0)
            kernel = kernel + correlate(combined, weighted)
        return kernel, None

    start = jnp.zeros((2, NX, NY, CZ), jnp.float32)
    kernel, _ = lax.scan(one_group, start, jnp.arange(N_STA, dtype=jnp.int32))
    return kernel
```

```python
import functools

import jax
import jax.numpy as jnp
from jax import lax
from jax.experimental import pallas as pl
from jax.experimental.pallas import tpu as pltpu
from jax.sharding import PartitionSpec as P

MESH = pl.DeviceIdType.MESH
F32 = jnp.float32
BF16 = jnp.bfloat16

C_NEAR = 8.0 / 12.0
TIME_STEP = 0.25
AMPLITUDE = 4.0
KERNEL_SCALE = 0.0625
STIFFNESS = 0.3

YY, YZ, XY, XX, XZ, ZZ = range(6)
STRESS_FROM = (1, 5, 3, 0, 4, 2)
VX, VY, VZ = range(3)
SIDES = (("gx", -1), ("gx", 1), ("gy", -1), ("gy", 1))
XLO, XHI, YLO, YHI = range(4)


def body(
    rec_hbm,
    src_hbm,
    mat_hbm,
    table_ref,
    res_ref,
    cell_ref,
    listed_ref,
    pick_ref,
    out_ref,
    stress,
    stress_y,
    vel,
    vel_y,
    weighted,
    mat,
    coef,
    rows_in,
    mine,
    other,
    gath,
    acc,
    parts,
    in_sem,
    h_send,
    h_recv,
    a_send,
    a_recv,
    b_sem,
    g_send,
    g_recv,
    r_send,
    r_recv,
):
    recs = stress.shape[0]
    steps = weighted.shape[0]
    tile_x = coef.shape[1]
    rows, depth = coef.shape[2], coef.shape[3]
    turns = listed_ref.shape[0]
    n_sta = parts.shape[0]
    n_col = gath.shape[0]
    gx, gy, sta = lax.axis_index("gx"), lax.axis_index("gy"), lax.axis_index("sta")
    n_gx, n_gy = lax.axis_size("gx"), lax.axis_size("gy")
    sx, sy = sta // 2, sta % 2
    pos = {"gx": (gx, n_gx), "gy": (gy, n_gy)}

    loads = [pltpu.make_async_copy(mat_hbm, mat, in_sem.at[0])]
    for c, src in enumerate(STRESS_FROM):
        loads.append(
            pltpu.make_async_copy(
                rec_hbm.at[0, :, 3 + src], stress.at[:, c, pl.ds(2, tile_x)], in_sem.at[1 + c]
            )
        )
    for c in range(3):
        loads.append(
            pltpu.make_async_copy(
                rec_hbm.at[0, :, c], vel.at[:, c, pl.ds(2, tile_x)], in_sem.at[7 + c]
            )
        )
    own_rows = pltpu.make_async_copy(
        src_hbm.at[0, :, :, pl.ds(2 * sx, 2)], rows_in.at[sx], in_sem.at[10]
    )
    for load in loads:
        load.start()
    own_rows.start()

    zero = jnp.zeros((rows, depth), F32)

    @pl.loop(0, recs)
    def _(r):
        for c in range(6):
            for row in (0, 1, tile_x + 2, tile_x + 3):
                stress[r, c, row] = zero
        for c in range(3):
            for row in (0, 1, tile_x + 2, tile_x + 3):
                vel[r, c, row] = zero
            for row in range(tile_x):
                stress_y[r, c, row] = zero
                vel_y[r, c, row] = zero

    barrier = pltpu.get_barrier_semaphore()

    def has(side):
        axis, step = SIDES[side]
        at, count = pos[axis]
        return at > 0 if step < 0 else at < count - 1

    for d in range(1, n_sta):
        pl.semaphore_signal(
            barrier, inc=1, device_id={"sta": (sta + d) % n_sta}, device_id_type=MESH
        )
    for side, (axis, step) in enumerate(SIDES):

        @pl.when(has(side))
        def _(axis=axis, step=step):
            pl.semaphore_signal(
                barrier, inc=1, device_id={axis: pos[axis][0] + step}, device_id_type=MESH
            )

    loads[0].wait()
    for x in range(tile_x):
        m = mat[x]
        b = jnp.zeros((rows, depth), F32)
        la = jnp.zeros((rows, depth), F32)
        sh = jnp.zeros((rows, depth), F32)
        for k in range(table_ref.shape[0]):
            hit = m == k
            b = jnp.where(hit, table_ref[k, 0], b)
            la = jnp.where(hit, table_ref[k, 1], la)
            sh = jnp.where(hit, table_ref[k, 2], sh)
        coef[0, x] = TIME_STEP * C_NEAR / b
        coef[1, x] = (TIME_STEP * STIFFNESS * C_NEAR) * la
        coef[2, x] = (TIME_STEP * STIFFNESS * C_NEAR) * sh

    @pl.loop(0, steps)
    def _(n):
        for c in range(6):
            for x in range(tile_x):
                weighted[n, c, x] = zero

    for load in loads[1:]:
        load.wait()
    peers = n_sta - 1
    for side in range(4):
        peers = peers + has(side).astype(jnp.int32)
    pl.semaphore_wait(barrier, peers)

    def halo(kind, side, r):
        axis, step = SIDES[side]
        at, count = pos[axis]
        to = jnp.clip(at + step, 0, count - 1)
        field, edge = ((stress, stress_y), (vel, vel_y))[kind]
        if axis == "gx":
            cs = pl.ds(XY if kind == 0 else 0, 3)
            src = field.at[r, cs, pl.ds(2 if step < 0 else tile_x, 2)]
            dst = field.at[r, cs, pl.ds(tile_x + 2 if step < 0 else 0, 2)]
        else:
            at_row = pl.ds(0 if step < 0 else rows - 2, 2)
            src = field.at[r, pl.ds(0, 3), pl.ds(2, tile_x), at_row]
            dst = edge.at[r, :, :, at_row]
        return pltpu.make_async_remote_copy(
            src_ref=src,
            dst_ref=dst,
            send_sem=h_send.at[kind, side, r],
            recv_sem=h_recv.at[kind, side, r],
            device_id={axis: to},
            device_id_type=MESH,
        )

    def send(kind, r):
        for side in range(4):

            @pl.when(has(side))
            def _(side=side):
                halo(kind, side, r).start()

    def arrive(kind, r):
        for side in range(4):

            @pl.when(has(side ^ 1))
            def _(side=side):
                halo(kind, side, r).wait_recv()

            @pl.when(has(side))
            def _(side=side):
                halo(kind, side, r).wait_send()

    @pl.loop(0, recs)
    def _(r):
        send(0, r)

    def row_copy(d):
        to = (sx + d) % n_col
        return pltpu.make_async_remote_copy(
            src_ref=src_hbm.at[0, :, :, pl.ds(2 * to, 2)],
            dst_ref=rows_in.at[sx],
            send_sem=a_send.at[d - 1],
            recv_sem=a_recv.at[d - 1],
            device_id={"sta": 2 * to + sy},
            device_id_type=MESH,
        )

    for d in range(1, n_col):
        row_copy(d).start()

    partner_copy = pltpu.make_async_remote_copy(
        src_ref=mine,
        dst_ref=other,
        send_sem=b_sem.at[0],
        recv_sem=b_sem.at[1],
        device_id={"sta": 2 * sx + 1 - sy},
        device_id_type=MESH,
    )

    def ring(k):
        step = 1 if k % 2 == 0 else n_col - 1
        to = (sx + step) % n_col
        slot = sx if k < 2 else (sx + n_col - step) % n_col
        part = pl.ds(0, turns * steps) if k < 2 else pl.ds((k - 2) * steps, steps)
        ref = gath.at[slot, part]
        return pltpu.make_async_remote_copy(
            src_ref=ref,
            dst_ref=ref,
            send_sem=g_send.at[k],
            recv_sem=g_recv.at[k],
            device_id={"sta": 2 * to + sy},
            device_id_type=MESH,
        )

    def pick_rows():
        own_rows.wait()
        for d in range(1, n_col):
            row_copy(d).wait()
        for t in range(turns):

            @pl.loop(0, steps)
            def _(n, t=t):
                p = pick_ref[t, n]
                keep = p % 2 == sy
                for c in range(6):
                    for j in range(2):
                        v = rows_in[p // 2, n, c, j]
                        mine[t * steps + n, c, j] = jnp.where(keep, v, jnp.zeros_like(v))

        partner_copy.start()

    def gather_rows():
        partner_copy.wait()

        @pl.loop(0, turns * steps)
        def _(q):
            for c in range(6):
                for j in range(2):
                    gath[sx, q, c, j] = mine[q, c, j] + other[q, c, j]

        ring(0).start()
        ring(1).start()

    def relay_rows():
        ring(0).wait()
        ring(1).wait()
        ring(2).start()
        ring(3).start()

    row_at = lax.broadcasted_iota(jnp.int32, (rows, depth), 0)
    lane_at = lax.broadcasted_iota(jnp.int32, (rows, depth), 1)
    first1, first2 = row_at < 1, row_at < 2
    last1, last2 = row_at >= rows - 1, row_at >= rows - 2
    src_at = lax.broadcasted_iota(jnp.int32, (2 * depth, depth), 0) % depth
    off = src_at - lax.broadcasted_iota(jnp.int32, (2 * depth, depth), 1)
    band = jnp.where(off == 1, 1.0, 0.0) - jnp.where(off == -1, 1.0, 0.0)
    band = band + 0.125 * (jnp.where(off == -2, 1.0, 0.0) - jnp.where(off == 2, 1.0, 0.0))
    band = band.astype(BF16)

    def diff_x(ref, r, c, x):
        near = ref[r, c, x + 3] - ref[r, c, x + 1]
        return near - 0.125 * (ref[r, c, x + 4] - ref[r, c, x])

    def diff_y(ref, edge, r, c, x):
        t, e = ref[r, c, x + 2], edge[r, c, x]
        up1 = pltpu.roll(jnp.where(first1, e, t), rows - 1, 0)
        up2 = pltpu.roll(jnp.where(first2, e, t), rows - 2, 0)
        dn1 = pltpu.roll(jnp.where(last1, e, t), 1, 0)
        dn2 = pltpu.roll(jnp.where(last2, e, t), 2, 0)
        return (up1 - dn1) - 0.125 * (up2 - dn2)

    def diff_z(ref, r, c):
        f = ref[r, c, pl.ds(2, tile_x)].reshape(tile_x * rows, depth)
        hi = f.astype(BF16)
        lo = (f - hi.astype(F32)).astype(BF16)
        both = jnp.concatenate([hi, lo], 1)
        d = jnp.dot(both, band, preferred_element_type=F32)
        return d.reshape(tile_x, rows, depth)

    def velocity(n, r):
        zx = diff_z(stress, r, XZ)
        zy = diff_z(stress, r, YZ)
        zz = diff_z(stress, r, ZZ)
        cell = cell_ref[0, r]
        cx = cell // (n_gy * rows) - gx * tile_x
        cy = cell % (n_gy * rows) - gy * rows
        amp = (AMPLITUDE / C_NEAR) * res_ref[0, r, n]
        spot = jnp.where((row_at == cy) & (lane_at == 0), amp, 0.0)
        for x in range(tile_x):
            b = coef[0, x]
            fx = diff_x(stress, r, XX, x) + diff_y(stress, stress_y, r, XY, x) + zx[x]
            fy = diff_x(stress, r, XY, x) + diff_y(stress, stress_y, r, YY, x) + zy[x]
            fz = diff_x(stress, r, XZ, x) + diff_y(stress, stress_y, r, YZ, x) + zz[x]
            fz = fz + spot * jnp.where(cx == x, 1.0, 0.0)
            vel[r, VX, x + 2] = vel[r, VX, x + 2] + b * fx
            vel[r, VY, x + 2] = vel[r, VY, x + 2] + b * fy
            vel[r, VZ, x + 2] = vel[r, VZ, x + 2] + b * fz

    def strain(n, r):
        zx = diff_z(vel, r, VX)
        zy = diff_z(vel, r, VY)
        zz = diff_z(vel, r, VZ)
        res = res_ref[0, r, n]
        for x in range(tile_x):
            la, mu = coef[1, x], coef[2, x]
            mu2 = mu + mu
            rxx = diff_x(vel, r, VX, x)
            ryy = diff_y(vel, vel_y, r, VY, x)
            rzz = zz[x]
            rxy = diff_y(vel, vel_y, r, VX, x) + diff_x(vel, r, VY, x)
            rxz = zx[x] + diff_x(vel, r, VZ, x)
            ryz = zy[x] + diff_y(vel, vel_y, r, VZ, x)
            tr = la * (rxx + ryy + rzz)
            put = ((XX, rxx), (YY, ryy), (ZZ, rzz), (XY, rxy), (XZ, rxz), (YZ, ryz))
            for k, (c, v) in enumerate(put):
                weighted[n, k, x] = weighted[n, k, x] + res * v
                if k < 3:
                    stress[r, c, x + 2] = stress[r, c, x + 2] + (tr + mu2 * v)
                else:
                    stress[r, c, x + 2] = stress[r, c, x + 2] + mu * v

    @pl.loop(0, steps)
    def _(n):
        @pl.loop(0, recs)
        def _(r):
            arrive(0, r)
            velocity(n, r)
            send(1, r)

        @pl.loop(0, recs)
        def _(r):
            arrive(1, r)
            strain(n, r)

            @pl.when(n < steps - 1)
            def _():
                send(0, r)

        pl.when(n == 2)(pick_rows)
        pl.when(n == 4)(gather_rows)
        pl.when(n == 6)(relay_rows)

    ring(2).wait()
    ring(3).wait()

    for x in range(tile_x):
        for k in range(2):
            acc[x, k] = zero

    scale = KERNEL_SCALE * C_NEAR

    @pl.loop(0, steps)
    def _(n):
        share = [listed_ref[t, n, sta].astype(F32) for t in range(turns)]
        for x in range(tile_x):
            comb = []
            for c in range(6):
                total = None
                for t in range(turns):
                    v = share[t] * gath[x // 2, t * steps + n, c, x % 2].astype(F32)
                    total = v if total is None else total + v
                comb.append(total)
            w = [weighted[n, k, x] for k in range(6)]
            lam = (comb[0] + comb[1] + comb[2]) * (w[0] + w[1] + w[2])
            mu = comb[0] * w[0]
            for c in range(1, 6):
                mu = mu + comb[c] * w[c]
            acc[x, 0] = acc[x, 0] + scale * lam
            acc[x, 1] = acc[x, 1] + (2.0 * scale) * mu

    def share_copy(d):
        to = (sta + d) % n_sta
        return pltpu.make_async_remote_copy(
            src_ref=acc.at[to],
            dst_ref=parts.at[d],
            send_sem=r_send.at[d],
            recv_sem=r_recv.at[d],
            device_id={"sta": to},
            device_id_type=MESH,
        )

    for d in range(1, n_sta):
        share_copy(d).start()
    for k in range(2):
        out_ref[k, 0] = acc[sta, k]
    for d in range(1, n_sta):
        share_copy(d).wait()
        for k in range(2):
            out_ref[k, 0] = out_ref[k, 0] + parts[d, k]


def local(rec_state, source_strain, material, material_table, residual, rec_cell, listed, src_pick):
    _, recs, _, tile_x, tile_y, depth = rec_state.shape
    steps = source_strain.shape[1]
    turns = listed.shape[0]
    n_sta = lax.axis_size("sta")
    n_col = n_sta // 2
    plane = (tile_y, depth)
    any_ = pl.BlockSpec(memory_space=pl.ANY)
    smem = pl.BlockSpec(memory_space=pltpu.SMEM)
    dma = pltpu.SemaphoreType.DMA
    return pl.pallas_call(
        body,
        out_shape=jax.ShapeDtypeStruct((2, 1, *plane), F32),
        in_specs=[any_, any_, any_, smem, smem, smem, smem, smem],
        out_specs=pl.BlockSpec(memory_space=pltpu.VMEM),
        scratch_shapes=[
            pltpu.VMEM((recs, 6, tile_x + 4, *plane), F32),
            pltpu.VMEM((recs, 3, tile_x, *plane), F32),
            pltpu.VMEM((recs, 3, tile_x + 4, *plane), F32),
            pltpu.VMEM((recs, 3, tile_x, *plane), F32),
            pltpu.VMEM((steps, 6, tile_x, *plane), F32),
            pltpu.VMEM((tile_x, *plane), jnp.int32),
            pltpu.VMEM((3, tile_x, *plane), F32),
            pltpu.VMEM((n_col, steps, 6, 2, *plane), BF16),
            pltpu.VMEM((turns * steps, 6, 2, *plane), BF16),
            pltpu.VMEM((turns * steps, 6, 2, *plane), BF16),
            pltpu.VMEM((n_col, turns * steps, 6, 2, *plane), BF16),
            pltpu.VMEM((tile_x, 2, *plane), F32),
            pltpu.VMEM((n_sta, 2, *plane), F32),
            dma((11,)),
            dma((2, 4, recs)),
            dma((2, 4, recs)),
            dma((n_col - 1,)),
            dma((n_col - 1,)),
            dma((2,)),
            dma((4,)),
            dma((4,)),
            dma((n_sta,)),
            dma((n_sta,)),
        ],
        compiler_params=pltpu.CompilerParams(
            collective_id=0, has_side_effects=True, vmem_limit_bytes=48 << 20
        ),
        name="kernels",
    )(rec_state, source_strain, material, material_table, residual, rec_cell, listed, src_pick)


def solution(mesh):
    in_specs = (
        P("sta", None, None, "gx", "gy", None),
        P("sta", None, None, "gx", "gy", None),
        P("gx", "gy", None),
        P(),
        P("sta", None, None),
        P("sta", None),
        P(),
        P(),
    )
    out_specs = P(None, ("gx", "sta"), "gy", None)
    return jax.shard_map(local, mesh=mesh, in_specs=in_specs, out_specs=out_specs, check_vma=False)
```

```python
import functools

import jax
import jax.numpy as jnp
from jax import lax
from jax.experimental import pallas as pl
from jax.experimental.pallas import tpu as pltpu
from jax.sharding import PartitionSpec as P

MESH = pl.DeviceIdType.MESH
F32 = jnp.float32
BF16 = jnp.bfloat16

C_NEAR = 8.0 / 12.0
TIME_STEP = 0.25
AMPLITUDE = 4.0
KERNEL_SCALE = 0.0625
STIFFNESS = 0.3

YY, YZ, XY, XX, XZ, ZZ = range(6)
STRESS_FROM = (1, 5, 3, 0, 4, 2)
VX, VY, VZ = range(3)
SIDES = (("gx", -1), ("gx", 1), ("gy", -1), ("gy", 1))
XLO, XHI, YLO, YHI = range(4)


def body(
    rec_hbm,
    src_hbm,
    mat_hbm,
    table_hbm,
    res_hbm,
    cell_hbm,
    listed_hbm,
    pick_hbm,
    out_ref,
    stress,
    stress_y,
    vel,
    vel_y,
    weighted,
    mat,
    coef,
    rows_in,
    mine,
    other,
    gath,
    acc,
    parts,
    table_ref,
    res_ref,
    cell_ref,
    listed_ref,
    pick_ref,
    in_sem,
    h_send,
    h_recv,
    a_send,
    a_recv,
    b_sem,
    g_send,
    g_recv,
    r_send,
    r_recv,
):
    recs = stress.shape[0]
    steps = weighted.shape[0]
    tile_x = coef.shape[1]
    rows, depth = coef.shape[2], coef.shape[3]
    turns = listed_ref.shape[0]
    n_sta = parts.shape[0]
    n_col = gath.shape[0]
    gx, gy, sta = lax.axis_index("gx"), lax.axis_index("gy"), lax.axis_index("sta")
    n_gx, n_gy = lax.axis_size("gx"), lax.axis_size("gy")
    sx, sy = sta // 2, sta % 2
    pos = {"gx": (gx, n_gx), "gy": (gy, n_gy)}

    loads = [pltpu.make_async_copy(mat_hbm, mat, in_sem.at[0])]
    for c, src in enumerate(STRESS_FROM):
        loads.append(
            pltpu.make_async_copy(
                rec_hbm.at[0, :, 3 + src], stress.at[:, c, pl.ds(2, tile_x)], in_sem.at[1 + c]
            )
        )
    for c in range(3):
        loads.append(
            pltpu.make_async_copy(
                rec_hbm.at[0, :, c], vel.at[:, c, pl.ds(2, tile_x)], in_sem.at[7 + c]
            )
        )
    own_rows = pltpu.make_async_copy(
        src_hbm.at[0, :, :, pl.ds(2 * sx, 2)], rows_in.at[sx], in_sem.at[10]
    )
    smalls = (
        (table_hbm, table_ref),
        (res_hbm, res_ref),
        (cell_hbm, cell_ref),
        (listed_hbm, listed_ref),
        (pick_hbm, pick_ref),
    )
    for k, (a, b) in enumerate(smalls):
        loads.insert(1 + k, pltpu.make_async_copy(a, b, in_sem.at[11 + k]))
    for load in loads:
        load.start()
    own_rows.start()

    zero = jnp.zeros((rows, depth), F32)

    @pl.loop(0, recs)
    def _(r):
        for c in range(6):
            for row in (0, 1, tile_x + 2, tile_x + 3):
                stress[r, c, row] = zero
        for c in range(3):
            for row in (0, 1, tile_x + 2, tile_x + 3):
                vel[r, c, row] = zero
            for row in range(tile_x):
                stress_y[r, c, row] = zero
                vel_y[r, c, row] = zero

    barrier = pltpu.get_barrier_semaphore()

    def has(side):
        axis, step = SIDES[side]
        at, count = pos[axis]
        return at > 0 if step < 0 else at < count - 1

    for d in range(1, n_sta):
        pl.semaphore_signal(
            barrier, inc=1, device_id={"sta": (sta + d) % n_sta}, device_id_type=MESH
        )
    for side, (axis, step) in enumerate(SIDES):

        @pl.when(has(side))
        def _(axis=axis, step=step):
            pl.semaphore_signal(
                barrier, inc=1, device_id={axis: pos[axis][0] + step}, device_id_type=MESH
            )

    for load in loads[:6]:
        load.wait()
    for x in range(tile_x):
        m = mat[x]
        b = jnp.zeros((rows, depth), F32)
        la = jnp.zeros((rows, depth), F32)
        sh = jnp.zeros((rows, depth), F32)
        for k in range(table_ref.shape[1]):
            hit = m == k
            b = jnp.where(hit, table_ref[0, k], b)
            la = jnp.where(hit, table_ref[1, k], la)
            sh = jnp.where(hit, table_ref[2, k], sh)
        coef[0, x] = TIME_STEP * C_NEAR / b
        coef[1, x] = (TIME_STEP * STIFFNESS * C_NEAR) * la
        coef[2, x] = (TIME_STEP * STIFFNESS * C_NEAR) * sh

    @pl.loop(0, steps)
    def _(n):
        for c in range(6):
            for x in range(tile_x):
                weighted[n, c, x] = zero

    for load in loads[6:]:
        load.wait()
    peers = n_sta - 1
    for side in range(4):
        peers = peers + has(side).astype(jnp.int32)
    pl.semaphore_wait(barrier, peers)

    def halo(kind, side, r):
        axis, step = SIDES[side]
        at, count = pos[axis]
        to = jnp.clip(at + step, 0, count - 1)
        field, edge = ((stress, stress_y), (vel, vel_y))[kind]
        if axis == "gx":
            cs = pl.ds(XY if kind == 0 else 0, 3)
            src = field.at[r, cs, pl.ds(2 if step < 0 else tile_x, 2)]
            dst = field.at[r, cs, pl.ds(tile_x + 2 if step < 0 else 0, 2)]
        else:
            at_row = pl.ds(0 if step < 0 else rows - 2, 2)
            src = field.at[r, pl.ds(0, 3), pl.ds(2, tile_x), at_row]
            dst = edge.at[r, :, :, at_row]
        return pltpu.make_async_remote_copy(
            src_ref=src,
            dst_ref=dst,
            send_sem=h_send.at[kind, side, r],
            recv_sem=h_recv.at[kind, side, r],
            device_id={axis: to},
            device_id_type=MESH,
        )

    def send(kind, r):
        for side in range(4):

            @pl.when(has(side))
            def _(side=side):
                halo(kind, side, r).start()

    def arrive(kind, r):
        for side in range(4):

            @pl.when(has(side ^ 1))
            def _(side=side):
                halo(kind, side, r).wait_recv()

            @pl.when(has(side))
            def _(side=side):
                halo(kind, side, r).wait_send()

    @pl.loop(0, recs)
    def _(r):
        send(0, r)

    def row_copy(d):
        to = (sx + d) % n_col
        return pltpu.make_async_remote_copy(
            src_ref=src_hbm.at[0, :, :, pl.ds(2 * to, 2)],
            dst_ref=rows_in.at[sx],
            send_sem=a_send.at[d - 1],
            recv_sem=a_recv.at[d - 1],
            device_id={"sta": 2 * to + sy},
            device_id_type=MESH,
        )

    for d in range(1, n_col):
        row_copy(d).start()

    partner_copy = pltpu.make_async_remote_copy(
        src_ref=mine,
        dst_ref=other,
        send_sem=b_sem.at[0],
        recv_sem=b_sem.at[1],
        device_id={"sta": 2 * sx + 1 - sy},
        device_id_type=MESH,
    )

    def ring(k):
        step = 1 if k % 2 == 0 else n_col - 1
        to = (sx + step) % n_col
        slot = sx if k < 2 else (sx + n_col - step) % n_col
        part = pl.ds(0, turns * steps) if k < 2 else pl.ds((k - 2) * steps, steps)
        ref = gath.at[slot, part]
        return pltpu.make_async_remote_copy(
            src_ref=ref,
            dst_ref=ref,
            send_sem=g_send.at[k],
            recv_sem=g_recv.at[k],
            device_id={"sta": 2 * to + sy},
            device_id_type=MESH,
        )

    def pick_rows():
        own_rows.wait()
        for d in range(1, n_col):
            row_copy(d).wait()
        for t in range(turns):

            @pl.loop(0, steps)
            def _(n, t=t):
                p = pick_ref[t, n]
                keep = p % 2 == sy
                for c in range(6):
                    for j in range(2):
                        v = rows_in[p // 2, n, c, j]
                        mine[t * steps + n, c, j] = jnp.where(keep, v, jnp.zeros_like(v))

        partner_copy.start()

    def gather_rows():
        partner_copy.wait()

        @pl.loop(0, turns * steps)
        def _(q):
            for c in range(6):
                for j in range(2):
                    gath[sx, q, c, j] = mine[q, c, j] + other[q, c, j]

        ring(0).start()
        ring(1).start()

    def relay_rows():
        ring(0).wait()
        ring(1).wait()
        ring(2).start()
        ring(3).start()

    row_at = lax.broadcasted_iota(jnp.int32, (rows, depth), 0)
    lane_at = lax.broadcasted_iota(jnp.int32, (rows, depth), 1)
    first1, first2 = row_at < 1, row_at < 2
    last1, last2 = row_at >= rows - 1, row_at >= rows - 2
    src_at = lax.broadcasted_iota(jnp.int32, (2 * depth, depth), 0) % depth
    off = src_at - lax.broadcasted_iota(jnp.int32, (2 * depth, depth), 1)
    band = jnp.where(off == 1, 1.0, 0.0) - jnp.where(off == -1, 1.0, 0.0)
    band = band + 0.125 * (jnp.where(off == -2, 1.0, 0.0) - jnp.where(off == 2, 1.0, 0.0))
    band = band.astype(BF16)

    def diff_x(ref, r, c, x):
        near = ref[r, c, x + 3] - ref[r, c, x + 1]
        return near - 0.125 * (ref[r, c, x + 4] - ref[r, c, x])

    def diff_y(ref, edge, r, c, x):
        t, e = ref[r, c, x + 2], edge[r, c, x]
        up1 = pltpu.roll(jnp.where(first1, e, t), rows - 1, 0)
        up2 = pltpu.roll(jnp.where(first2, e, t), rows - 2, 0)
        dn1 = pltpu.roll(jnp.where(last1, e, t), 1, 0)
        dn2 = pltpu.roll(jnp.where(last2, e, t), 2, 0)
        return (up1 - dn1) - 0.125 * (up2 - dn2)

    def diff_z(ref, r, c):
        f = ref[r, c, pl.ds(2, tile_x)].reshape(tile_x * rows, depth)
        hi = f.astype(BF16)
        lo = (f - hi.astype(F32)).astype(BF16)
        both = jnp.concatenate([hi, lo], 1)
        d = jnp.dot(both, band, preferred_element_type=F32)
        return d.reshape(tile_x, rows, depth)

    def velocity(n, r):
        zx = diff_z(stress, r, XZ)
        zy = diff_z(stress, r, YZ)
        zz = diff_z(stress, r, ZZ)
        cell = cell_ref[0, r]
        cx = cell // (n_gy * rows) - gx * tile_x
        cy = cell % (n_gy * rows) - gy * rows
        amp = (AMPLITUDE / C_NEAR) * res_ref[0, r, n]
        spot = jnp.where((row_at == cy) & (lane_at == 0), amp, 0.0)
        for x in range(tile_x):
            b = coef[0, x]
            fx = diff_x(stress, r, XX, x) + diff_y(stress, stress_y, r, XY, x) + zx[x]
            fy = diff_x(stress, r, XY, x) + diff_y(stress, stress_y, r, YY, x) + zy[x]
            fz = diff_x(stress, r, XZ, x) + diff_y(stress, stress_y, r, YZ, x) + zz[x]
            fz = fz + spot * jnp.where(cx == x, 1.0, 0.0)
            vel[r, VX, x + 2] = vel[r, VX, x + 2] + b * fx
            vel[r, VY, x + 2] = vel[r, VY, x + 2] + b * fy
            vel[r, VZ, x + 2] = vel[r, VZ, x + 2] + b * fz

    def strain(n, r):
        zx = diff_z(vel, r, VX)
        zy = diff_z(vel, r, VY)
        zz = diff_z(vel, r, VZ)
        res = res_ref[0, r, n]
        for x in range(tile_x):
            la, mu = coef[1, x], coef[2, x]
            mu2 = mu + mu
            rxx = diff_x(vel, r, VX, x)
            ryy = diff_y(vel, vel_y, r, VY, x)
            rzz = zz[x]
            rxy = diff_y(vel, vel_y, r, VX, x) + diff_x(vel, r, VY, x)
            rxz = zx[x] + diff_x(vel, r, VZ, x)
            ryz = zy[x] + diff_y(vel, vel_y, r, VZ, x)
            tr = la * (rxx + ryy + rzz)
            put = ((XX, rxx), (YY, ryy), (ZZ, rzz), (XY, rxy), (XZ, rxz), (YZ, ryz))
            for k, (c, v) in enumerate(put):
                weighted[n, k, x] = weighted[n, k, x] + res * v
                if k < 3:
                    stress[r, c, x + 2] = stress[r, c, x + 2] + (tr + mu2 * v)
                else:
                    stress[r, c, x + 2] = stress[r, c, x + 2] + mu * v

    @pl.loop(0, steps)
    def _(n):
        @pl.loop(0, recs)
        def _(r):
            arrive(0, r)
            velocity(n, r)
            send(1, r)

        @pl.loop(0, recs)
        def _(r):
            arrive(1, r)
            strain(n, r)

            @pl.when(n < steps - 1)
            def _():
                send(0, r)

        pl.when(n == 2)(pick_rows)
        pl.when(n == 4)(gather_rows)
        pl.when(n == 6)(relay_rows)

    ring(2).wait()
    ring(3).wait()

    for x in range(tile_x):
        for k in range(2):
            acc[x, k] = zero

    scale = KERNEL_SCALE * C_NEAR

    @pl.loop(0, steps)
    def _(n):
        share = [listed_ref[t, n, sta].astype(F32) for t in range(turns)]
        for x in range(tile_x):
            comb = []
            for c in range(6):
                total = None
                for t in range(turns):
                    v = share[t] * gath[x // 2, t * steps + n, c, x % 2].astype(F32)
                    total = v if total is None else total + v
                comb.append(total)
            w = [weighted[n, k, x] for k in range(6)]
            lam = (comb[0] + comb[1] + comb[2]) * (w[0] + w[1] + w[2])
            mu = comb[0] * w[0]
            for c in range(1, 6):
                mu = mu + comb[c] * w[c]
            acc[x, 0] = acc[x, 0] + scale * lam
            acc[x, 1] = acc[x, 1] + (2.0 * scale) * mu

    def share_copy(d):
        to = (sta + d) % n_sta
        return pltpu.make_async_remote_copy(
            src_ref=acc.at[to],
            dst_ref=parts.at[d],
            send_sem=r_send.at[d],
            recv_sem=r_recv.at[d],
            device_id={"sta": to},
            device_id_type=MESH,
        )

    for d in range(1, n_sta):
        share_copy(d).start()
    for k in range(2):
        out_ref[k, 0] = acc[sta, k]
    for d in range(1, n_sta):
        share_copy(d).wait()
        for k in range(2):
            out_ref[k, 0] = out_ref[k, 0] + parts[d, k]


def local(rec_state, source_strain, material, material_table, residual, rec_cell, listed, src_pick):
    _, recs, _, tile_x, tile_y, depth = rec_state.shape
    steps = source_strain.shape[1]
    turns = listed.shape[0]
    n_sta = lax.axis_size("sta")
    n_col = n_sta // 2
    plane = (tile_y, depth)
    hbm = pl.BlockSpec(memory_space=pltpu.HBM)
    table = material_table.T
    smalls = (table, residual, rec_cell, listed, src_pick)
    dma = pltpu.SemaphoreType.DMA
    return pl.pallas_call(
        body,
        out_shape=jax.ShapeDtypeStruct((2, 1, *plane), F32),
        in_specs=[hbm] * 8,
        out_specs=pl.BlockSpec(memory_space=pltpu.VMEM),
        scratch_shapes=[
            pltpu.VMEM((recs, 6, tile_x + 4, *plane), F32),
            pltpu.VMEM((recs, 3, tile_x, *plane), F32),
            pltpu.VMEM((recs, 3, tile_x + 4, *plane), F32),
            pltpu.VMEM((recs, 3, tile_x, *plane), F32),
            pltpu.VMEM((steps, 6, tile_x, *plane), F32),
            pltpu.VMEM((tile_x, *plane), jnp.int32),
            pltpu.VMEM((3, tile_x, *plane), F32),
            pltpu.VMEM((n_col, steps, 6, 2, *plane), BF16),
            pltpu.VMEM((turns * steps, 6, 2, *plane), BF16),
            pltpu.VMEM((turns * steps, 6, 2, *plane), BF16),
            pltpu.VMEM((n_col, turns * steps, 6, 2, *plane), BF16),
            pltpu.VMEM((tile_x, 2, *plane), F32),
            pltpu.VMEM((n_sta, 2, *plane), F32),
            *[pltpu.SMEM(a.shape, a.dtype) for a in smalls],
            dma((16,)),
            dma((2, 4, recs)),
            dma((2, 4, recs)),
            dma((n_col - 1,)),
            dma((n_col - 1,)),
            dma((2,)),
            dma((4,)),
            dma((4,)),
            dma((n_sta,)),
            dma((n_sta,)),
        ],
        compiler_params=pltpu.CompilerParams(
            collective_id=0, has_side_effects=True
        ),
        name="kernels",
    )(rec_state, source_strain, material, *smalls)


def solution(mesh):
    in_specs = (
        P("sta", None, None, "gx", "gy", None),
        P("sta", None, None, "gx", "gy", None),
        P("gx", "gy", None),
        P(),
        P("sta", None, None),
        P("sta", None),
        P(),
        P(),
    )
    out_specs = P(None, ("gx", "sta"), "gy", None)
    return jax.shard_map(local, mesh=mesh, in_specs=in_specs, out_specs=out_specs, check_vma=False)
```

```python
import functools

import jax
import jax.numpy as jnp
from jax import lax
from jax.experimental import pallas as pl
from jax.experimental.pallas import tpu as pltpu
from jax.sharding import PartitionSpec as P

MESH = pl.DeviceIdType.MESH
F32 = jnp.float32
BF16 = jnp.bfloat16

C_NEAR = 8.0 / 12.0
TIME_STEP = 0.25
AMPLITUDE = 4.0
KERNEL_SCALE = 0.0625
STIFFNESS = 0.3

YY, YZ, XY, XX, XZ, ZZ = range(6)
STRESS_FROM = (1, 5, 3, 0, 4, 2)
VX, VY, VZ = range(3)
WAYS = ((-1, 0), (1, 0), (0, -1), (0, 1), (-1, -1), (-1, 1), (1, -1), (1, 1))
BACK = (1, 0, 3, 2, 7, 6, 5, 4)


def body(
    rec_hbm,
    src_hbm,
    mat_hbm,
    table_hbm,
    res_hbm,
    cell_hbm,
    listed_hbm,
    pick_hbm,
    out_ref,
    stress,
    stress_y,
    vel,
    vel_y,
    weighted,
    mat,
    mat_y,
    coef,
    coef_y,
    rows_in,
    mine,
    other,
    gath,
    acc,
    parts,
    table_ref,
    res_ref,
    cell_ref,
    listed_ref,
    pick_ref,
    in_sem,
    m_send,
    m_recv,
    i_send,
    i_recv,
    h_send,
    h_recv,
    a_send,
    a_recv,
    b_sem,
    g_send,
    g_recv,
    r_send,
    r_recv,
):
    recs = stress.shape[0]
    steps = weighted.shape[0]
    tile_x, rows, depth = coef_y.shape[1:]
    turns = listed_ref.shape[0]
    n_sta = parts.shape[0]
    n_col = gath.shape[0]
    gx, gy, sta = lax.axis_index("gx"), lax.axis_index("gy"), lax.axis_index("sta")
    n_gx, n_gy = lax.axis_size("gx"), lax.axis_size("gy")
    sx, sy = sta // 2, sta % 2

    loads = [pltpu.make_async_copy(mat_hbm, mat.at[pl.ds(2, tile_x)], in_sem.at[0])]
    for c, src in enumerate(STRESS_FROM):
        loads.append(
            pltpu.make_async_copy(
                rec_hbm.at[0, :, 3 + src], stress.at[:, c, pl.ds(2, tile_x)], in_sem.at[1 + c]
            )
        )
    for c in range(3):
        loads.append(
            pltpu.make_async_copy(
                rec_hbm.at[0, :, c], vel.at[1, :, c, pl.ds(4, tile_x)], in_sem.at[7 + c]
            )
        )
    own_rows = pltpu.make_async_copy(
        src_hbm.at[0, :, :, pl.ds(2 * sx, 2)], rows_in.at[sx], in_sem.at[10]
    )
    smalls = (
        (table_hbm, table_ref),
        (res_hbm, res_ref),
        (cell_hbm, cell_ref),
        (listed_hbm, listed_ref),
        (pick_hbm, pick_ref),
    )
    for k, (a, b) in enumerate(smalls):
        loads.insert(1 + k, pltpu.make_async_copy(a, b, in_sem.at[11 + k]))
    for load in loads:
        load.start()
    own_rows.start()

    zero = jnp.zeros((rows, depth), F32)
    none = jnp.full((rows, depth), -1, jnp.int32)
    for row in (0, 1, tile_x + 2, tile_x + 3):
        mat[row] = none
    for row in range(tile_x):
        mat_y[row] = none

    @pl.loop(0, recs)
    def _(r):
        for c in range(6):
            for row in (0, 1, tile_x + 2, tile_x + 3):
                stress[r, c, row] = zero
        for c in range(3):
            for row in range(tile_x):
                stress_y[r, c, row] = zero
            for p in range(2):
                for row in range(4):
                    vel[p, r, c, row] = zero
                    vel[p, r, c, tile_x + 4 + row] = zero
                for row in range(tile_x + 4):
                    vel_y[p, r, c, row] = zero

    barrier = pltpu.get_barrier_semaphore()

    def has(way):
        dx, dy = WAYS[way]
        ok = None
        for d, at, count in ((dx, gx, n_gx), (dy, gy, n_gy)):
            if d:
                one = at > 0 if d < 0 else at < count - 1
                ok = one if ok is None else ok & one
        return ok

    def device(way):
        dx, dy = WAYS[way]
        return {"gx": jnp.clip(gx + dx, 0, n_gx - 1), "gy": jnp.clip(gy + dy, 0, n_gy - 1)}

    for d in range(1, n_sta):
        pl.semaphore_signal(
            barrier, inc=1, device_id={"sta": (sta + d) % n_sta}, device_id_type=MESH
        )
    peers = n_sta - 1
    for way in range(8):

        @pl.when(has(way))
        def _(way=way):
            pl.semaphore_signal(barrier, inc=1, device_id=device(way), device_id_type=MESH)

        peers = peers + has(way).astype(jnp.int32)

    @pl.loop(0, steps)
    def _(n):
        for c in range(6):
            for x in range(tile_x):
                weighted[n, c, x] = zero

    for load in loads:
        load.wait()
    pl.semaphore_wait(barrier, peers)

    def part(d, low, high):
        return low if d < 0 else high

    def mat_copy(way):
        dx, dy = WAYS[way]
        if dx:
            src = mat.at[pl.ds(part(dx, 2, tile_x), 2)]
            dst = mat.at[pl.ds(part(dx, tile_x + 2, 0), 2)]
        else:
            at_row = pl.ds(part(dy, 0, rows - 2), 2)
            src, dst = mat.at[pl.ds(2, tile_x), at_row], mat_y.at[:, at_row]
        return pltpu.make_async_remote_copy(
            src_ref=src,
            dst_ref=dst,
            send_sem=m_send.at[way],
            recv_sem=m_recv.at[way],
            device_id=device(way),
            device_id_type=MESH,
        )

    def stress_copy(way, r):
        dx, dy = WAYS[way]
        if dx:
            src = stress.at[r, pl.ds(XY, 3), pl.ds(part(dx, 2, tile_x), 2)]
            dst = stress.at[r, pl.ds(XY, 3), pl.ds(part(dx, tile_x + 2, 0), 2)]
        else:
            at_row = pl.ds(part(dy, 0, rows - 2), 2)
            src = stress.at[r, pl.ds(0, 3), pl.ds(2, tile_x), at_row]
            dst = stress_y.at[r, :, :, at_row]
        return pltpu.make_async_remote_copy(
            src_ref=src,
            dst_ref=dst,
            send_sem=i_send.at[way, r],
            recv_sem=i_recv.at[way, r],
            device_id=device(way),
            device_id_type=MESH,
        )

    def vel_copy(way, p, r):
        dx, dy = WAYS[way]
        if dx and dy:
            at_row = pl.ds(part(dy, 0, rows - 2), 2)
            src = vel.at[p, r, pl.ds(0, 2), pl.ds(part(dx, 4, tile_x + 2), 2), at_row]
            dst = vel_y.at[p, r, pl.ds(0, 2), pl.ds(part(dx, tile_x + 2, 0), 2), at_row]
        elif dx:
            src = vel.at[p, r, :, pl.ds(part(dx, 4, tile_x), 4)]
            dst = vel.at[p, r, :, pl.ds(part(dx, tile_x + 4, 0), 4)]
        else:
            at_row = pl.ds(part(dy, 0, rows - 4), 4)
            src = vel.at[p, r, :, pl.ds(4, tile_x), at_row]
            dst = vel_y.at[p, r, :, pl.ds(2, tile_x), at_row]
        return pltpu.make_async_remote_copy(
            src_ref=src,
            dst_ref=dst,
            send_sem=h_send.at[p, way, r],
            recv_sem=h_recv.at[p, way, r],
            device_id=device(way),
            device_id_type=MESH,
        )

    def send(copy, ways, *at):
        for way in ways:

            @pl.when(has(way))
            def _(way=way):
                copy(way, *at).start()

    def arrive(copy, ways, *at):
        for way in ways:

            @pl.when(has(BACK[way]))
            def _(way=way):
                copy(way, *at).wait_recv()

            @pl.when(has(way))
            def _(way=way):
                copy(way, *at).wait_send()

    sides, corners = range(4), range(4, 8)

    @pl.loop(0, recs)
    def _(r):
        send(stress_copy, sides, r)

    send(mat_copy, sides)

    def row_copy(d):
        to = (sx + d) % n_col
        return pltpu.make_async_remote_copy(
            src_ref=src_hbm.at[0, :, :, pl.ds(2 * to, 2)],
            dst_ref=rows_in.at[sx],
            send_sem=a_send.at[d - 1],
            recv_sem=a_recv.at[d - 1],
            device_id={"sta": 2 * to + sy},
            device_id_type=MESH,
        )

    for d in range(1, n_col):
        row_copy(d).start()

    partner_copy = pltpu.make_async_remote_copy(
        src_ref=mine,
        dst_ref=other,
        send_sem=b_sem.at[0],
        recv_sem=b_sem.at[1],
        device_id={"sta": 2 * sx + 1 - sy},
        device_id_type=MESH,
    )

    def ring(k):
        step = 1 if k % 2 == 0 else n_col - 1
        to = (sx + step) % n_col
        slot = sx if k < 2 else (sx + n_col - step) % n_col
        part = pl.ds(0, turns * steps) if k < 2 else pl.ds((k - 2) * steps, steps)
        ref = gath.at[slot, part]
        return pltpu.make_async_remote_copy(
            src_ref=ref,
            dst_ref=ref,
            send_sem=g_send.at[k],
            recv_sem=g_recv.at[k],
            device_id={"sta": 2 * to + sy},
            device_id_type=MESH,
        )

    def pick_rows():
        own_rows.wait()
        for d in range(1, n_col):
            row_copy(d).wait()
        for t in range(turns):

            @pl.loop(0, steps)
            def _(n, t=t):
                p = pick_ref[t, n]
                keep = p % 2 == sy
                for c in range(6):
                    for j in range(2):
                        v = rows_in[p // 2, n, c, j]
                        mine[t * steps + n, c, j] = jnp.where(keep, v, jnp.zeros_like(v))

        partner_copy.start()

    def gather_rows():
        partner_copy.wait()

        @pl.loop(0, turns * steps)
        def _(q):
            for c in range(6):
                for j in range(2):
                    gath[sx, q, c, j] = mine[q, c, j] + other[q, c, j]

        ring(0).start()
        ring(1).start()

    def relay_rows():
        ring(0).wait()
        ring(1).wait()
        ring(2).start()
        ring(3).start()

    row_at = lax.broadcasted_iota(jnp.int32, (rows, depth), 0)
    lane_at = lax.broadcasted_iota(jnp.int32, (rows, depth), 1)
    first1, first2 = row_at < 1, row_at < 2
    last1, last2 = row_at >= rows - 1, row_at >= rows - 2
    src_at = lax.broadcasted_iota(jnp.int32, (2 * depth, depth), 0) % depth
    off = src_at - lax.broadcasted_iota(jnp.int32, (2 * depth, depth), 1)
    band = jnp.where(off == 1, 1.0, 0.0) - jnp.where(off == -1, 1.0, 0.0)
    band = band + 0.125 * (jnp.where(off == -2, 1.0, 0.0) - jnp.where(off == 2, 1.0, 0.0))
    band = band.astype(BF16)

    def diff_x(get, c, x):
        return (get(c, x + 1) - get(c, x - 1)) - 0.125 * (get(c, x + 2) - get(c, x - 2))

    def diff_y(t, e):
        up1 = pltpu.roll(jnp.where(first1, e, t), rows - 1, 0)
        up2 = pltpu.roll(jnp.where(first2, e, t), rows - 2, 0)
        dn1 = pltpu.roll(jnp.where(last1, e, t), 1, 0)
        dn2 = pltpu.roll(jnp.where(last2, e, t), 2, 0)
        return (up1 - dn1) - 0.125 * (up2 - dn2)

    def diff_z(f):
        planes = f.shape[0]
        f = f.reshape(planes * rows, depth)
        hi = f.astype(BF16)
        lo = (f - hi.astype(F32)).astype(BF16)
        both = jnp.concatenate([hi, lo], 1)
        d = jnp.dot(both, band, preferred_element_type=F32)
        return d.reshape(planes, rows, depth)

    tile = range(tile_x)

    def tables():
        def look(m, k):
            v = jnp.zeros((rows, depth), F32)
            for j in range(table_ref.shape[1]):
                v = jnp.where(m == j, table_ref[k, j], v)
            return v

        unit = TIME_STEP * STIFFNESS * C_NEAR
        for x in range(tile_x + 4):
            for k in (1, 2):
                coef[k, x] = unit * look(mat[x], k)
        for x in tile:
            for k in (1, 2):
                coef_y[k - 1, x] = unit * look(mat_y[x], k)

    def buoyancy():
        for x in tile:
            m = mat[x + 2]
            v = jnp.ones((rows, depth), F32)
            for j in range(table_ref.shape[1]):
                v = jnp.where(m == j, table_ref[0, j], v)
            coef[0, x + 2] = TIME_STEP * C_NEAR / v

    def velocity(n, p, r):
        def s(c, x):
            return stress[r, c, x + 2]

        def e(c, x):
            return stress_y[r, c, x]

        zx, zy, zz = (diff_z(stress[r, c, pl.ds(2, tile_x)]) for c in (XZ, YZ, ZZ))
        cell = cell_ref[0, r]
        cx = cell // (n_gy * rows) - gx * tile_x
        cy = cell % (n_gy * rows) - gy * rows
        amp = (AMPLITUDE / C_NEAR) * res_ref[0, r, n]
        spot = jnp.where((row_at == cy) & (lane_at == 0), amp, 0.0)
        for x in tile:
            b = coef[0, x + 2]
            fx = diff_x(s, XX, x) + diff_y(s(XY, x), e(XY, x)) + zx[x]
            fy = diff_x(s, XY, x) + diff_y(s(YY, x), e(YY, x)) + zy[x]
            fz = diff_x(s, XZ, x) + diff_y(s(YZ, x), e(YZ, x)) + zz[x]
            fz = fz + spot * jnp.where(cx == x, 1.0, 0.0)
            for c, f in ((VX, fx), (VY, fy), (VZ, fz)):
                vel[p, r, c, x + 4] = vel[1 - p, r, c, x + 4] + b * f

    def strain(n, p, r):
        def v(c, x):
            return vel[p, r, c, x + 4]

        def e(c, x):
            return vel_y[p, r, c, x + 2]

        zx, zy, zz = (diff_z(vel[p, r, c, pl.ds(4, tile_x)]) for c in (VX, VY, VZ))
        res = res_ref[0, r, n]
        for x in tile:
            la, mu = coef[1, x + 2], coef[2, x + 2]
            mu2 = mu + mu
            rxx = diff_x(v, VX, x)
            ryy = diff_y(v(VY, x), e(VY, x))
            rzz = zz[x]
            rxy = diff_y(v(VX, x), e(VX, x)) + diff_x(v, VY, x)
            rxz = zx[x] + diff_x(v, VZ, x)
            ryz = zy[x] + diff_y(v(VZ, x), e(VZ, x))
            tr = la * (rxx + ryy + rzz)
            put = ((XX, rxx), (YY, ryy), (ZZ, rzz), (XY, rxy), (XZ, rxz), (YZ, ryz))
            for k, (c, d) in enumerate(put):
                weighted[n, k, x] = weighted[n, k, x] + res * d
                step = tr + mu2 * d if k < 3 else mu * d
                stress[r, c, x + 2] = stress[r, c, x + 2] + step

    def strain_edges(p, r):
        def v(c, x):
            return vel[p, r, c, x + 4]

        def e(c, x):
            return vel_y[p, r, c, x + 2]

        for low in (-2, tile_x):
            zx, zz = (diff_z(vel[p, r, c, pl.ds(low + 4, 2)]) for c in (VX, VZ))
            for k in range(2):
                x = low + k
                la, mu = coef[1, x + 2], coef[2, x + 2]
                rxx = diff_x(v, VX, x)
                ryy = diff_y(v(VY, x), e(VY, x))
                rxy = diff_y(v(VX, x), e(VX, x)) + diff_x(v, VY, x)
                rxz = zx[k] + diff_x(v, VZ, x)
                sxx = la * (rxx + ryy + zz[k]) + (mu + mu) * rxx
                for c, step in ((XX, sxx), (XY, mu * rxy), (XZ, mu * rxz)):
                    stress[r, c, x + 2] = stress[r, c, x + 2] + step
        zy, zz = (diff_z(vel_y[p, r, c, pl.ds(2, tile_x)]) for c in (VY, VZ))
        for x in tile:
            la, mu = coef_y[0, x], coef_y[1, x]
            rxx = diff_x(e, VX, x)
            ryy = diff_y(e(VY, x), v(VY, x))
            rxy = diff_y(e(VX, x), v(VX, x)) + diff_x(e, VY, x)
            ryz = zy[x] + diff_y(e(VZ, x), v(VZ, x))
            syy = la * (rxx + ryy + zz[x]) + (mu + mu) * ryy
            for c, step in ((YY, syy), (XY, mu * rxy), (YZ, mu * ryz)):
                stress_y[r, c, x] = stress_y[r, c, x] + step

    buoyancy()

    @pl.loop(0, recs)
    def _(r):
        arrive(stress_copy, sides, r)
        velocity(0, 0, r)
        send(vel_copy, range(8), 0, r)

    arrive(mat_copy, sides)
    tables()

    @pl.loop(0, steps)
    def _(n):
        p = n % 2

        @pl.loop(0, recs)
        def _(r):
            arrive(vel_copy, sides, p, r)
            strain(n, p, r)
            arrive(vel_copy, corners, p, r)

            @pl.when(n < steps - 1)
            def _():
                strain_edges(p, r)
                velocity(n + 1, 1 - p, r)
                send(vel_copy, range(8), 1 - p, r)

        pl.when(n == 2)(pick_rows)
        pl.when(n == 4)(gather_rows)
        pl.when(n == 6)(relay_rows)

    ring(2).wait()
    ring(3).wait()

    for x in range(tile_x):
        for k in range(2):
            acc[x, k] = zero

    scale = KERNEL_SCALE * C_NEAR

    @pl.loop(0, steps)
    def _(n):
        share = [listed_ref[t, n, sta].astype(F32) for t in range(turns)]
        for x in range(tile_x):
            comb = []
            for c in range(6):
                total = None
                for t in range(turns):
                    v = share[t] * gath[x // 2, t * steps + n, c, x % 2].astype(F32)
                    total = v if total is None else total + v
                comb.append(total)
            w = [weighted[n, k, x] for k in range(6)]
            lam = (comb[0] + comb[1] + comb[2]) * (w[0] + w[1] + w[2])
            mu = comb[0] * w[0]
            for c in range(1, 6):
                mu = mu + comb[c] * w[c]
            acc[x, 0] = acc[x, 0] + scale * lam
            acc[x, 1] = acc[x, 1] + (2.0 * scale) * mu

    def share_copy(d):
        to = (sta + d) % n_sta
        return pltpu.make_async_remote_copy(
            src_ref=acc.at[to],
            dst_ref=parts.at[d],
            send_sem=r_send.at[d],
            recv_sem=r_recv.at[d],
            device_id={"sta": to},
            device_id_type=MESH,
        )

    for d in range(1, n_sta):
        share_copy(d).start()
    for k in range(2):
        out_ref[k, 0] = acc[sta, k]
    for d in range(1, n_sta):
        share_copy(d).wait()
        for k in range(2):
            out_ref[k, 0] = out_ref[k, 0] + parts[d, k]


def local(rec_state, source_strain, material, material_table, residual, rec_cell, listed, src_pick):
    _, recs, _, tile_x, tile_y, depth = rec_state.shape
    steps = source_strain.shape[1]
    turns = listed.shape[0]
    n_sta = lax.axis_size("sta")
    n_col = n_sta // 2
    plane = (tile_y, depth)
    hbm = pl.BlockSpec(memory_space=pltpu.HBM)
    table = material_table.T
    smalls = (table, residual, rec_cell, listed, src_pick)
    dma = pltpu.SemaphoreType.DMA
    return pl.pallas_call(
        body,
        out_shape=jax.ShapeDtypeStruct((2, 1, *plane), F32),
        in_specs=[hbm] * 8,
        out_specs=pl.BlockSpec(memory_space=pltpu.VMEM),
        scratch_shapes=[
            pltpu.VMEM((recs, 6, tile_x + 4, *plane), F32),
            pltpu.VMEM((recs, 3, tile_x, *plane), F32),
            pltpu.VMEM((2, recs, 3, tile_x + 8, *plane), F32),
            pltpu.VMEM((2, recs, 3, tile_x + 4, *plane), F32),
            pltpu.VMEM((steps, 6, tile_x, *plane), F32),
            pltpu.VMEM((tile_x + 4, *plane), jnp.int32),
            pltpu.VMEM((tile_x, *plane), jnp.int32),
            pltpu.VMEM((3, tile_x + 4, *plane), F32),
            pltpu.VMEM((2, tile_x, *plane), F32),
            pltpu.VMEM((n_col, steps, 6, 2, *plane), BF16),
            pltpu.VMEM((turns * steps, 6, 2, *plane), BF16),
            pltpu.VMEM((turns * steps, 6, 2, *plane), BF16),
            pltpu.VMEM((n_col, turns * steps, 6, 2, *plane), BF16),
            pltpu.VMEM((tile_x, 2, *plane), F32),
            pltpu.VMEM((n_sta, 2, *plane), F32),
            *[pltpu.SMEM(a.shape, a.dtype) for a in smalls],
            dma((16,)),
            dma((4,)),
            dma((4,)),
            dma((4, recs)),
            dma((4, recs)),
            dma((2, 8, recs)),
            dma((2, 8, recs)),
            dma((n_col - 1,)),
            dma((n_col - 1,)),
            dma((2,)),
            dma((4,)),
            dma((4,)),
            dma((n_sta,)),
            dma((n_sta,)),
        ],
        compiler_params=pltpu.CompilerParams(
            collective_id=0, has_side_effects=True
        ),
        name="kernels",
    )(rec_state, source_strain, material, *smalls)


def solution(mesh):
    in_specs = (
        P("sta", None, None, "gx", "gy", None),
        P("sta", None, None, "gx", "gy", None),
        P("gx", "gy", None),
        P(),
        P("sta", None, None),
        P("sta", None),
        P(),
        P(),
    )
    out_specs = P(None, ("gx", "sta"), "gy", None)
    return jax.shard_map(local, mesh=mesh, in_specs=in_specs, out_specs=out_specs, check_vma=False)
```

```python
import functools

import jax
import jax.numpy as jnp
from jax import lax
from jax.experimental import pallas as pl
from jax.experimental.pallas import tpu as pltpu
from jax.sharding import PartitionSpec as P

MESH = pl.DeviceIdType.MESH
F32 = jnp.float32
BF16 = jnp.bfloat16

C_NEAR = 8.0 / 12.0
TIME_STEP = 0.25
AMPLITUDE = 4.0
KERNEL_SCALE = 0.0625
STIFFNESS = 0.3

YY, YZ, XY, XX, XZ, ZZ = range(6)
STRESS_FROM = (1, 5, 3, 0, 4, 2)
VX, VY, VZ = range(3)
WAYS = ((-1, 0), (1, 0), (0, -1), (0, 1), (-1, -1), (-1, 1), (1, -1), (1, 1), (-1, 0), (1, 0))
BACK = (1, 0, 3, 2, 7, 6, 5, 4, 9, 8)
FAR = 2


def body(
    rec_hbm,
    src_hbm,
    mat_hbm,
    table_hbm,
    res_hbm,
    cell_hbm,
    listed_hbm,
    pick_hbm,
    out_ref,
    stress,
    stress_y,
    vel,
    vel_y,
    far_out,
    far_in,
    weighted,
    mat,
    mat_y,
    coef,
    coef_y,
    rows_in,
    mine,
    other,
    gath,
    acc,
    parts,
    table_ref,
    res_ref,
    cell_ref,
    listed_ref,
    pick_ref,
    in_sem,
    m_send,
    m_recv,
    i_send,
    i_recv,
    h_send,
    h_recv,
    a_send,
    a_recv,
    b_send,
    b_recv,
    g_send,
    g_recv,
    r_send,
    r_recv,
):
    recs = stress.shape[0]
    steps = weighted.shape[0]
    tile_x, rows, depth = coef_y.shape[1:]
    turns = listed_ref.shape[0]
    n_sta = parts.shape[0]
    n_col = gath.shape[0]
    gx, gy, sta = lax.axis_index("gx"), lax.axis_index("gy"), lax.axis_index("sta")
    n_gx, n_gy = lax.axis_size("gx"), lax.axis_size("gy")
    sx, sy = sta // 2, sta % 2

    loads = [pltpu.make_async_copy(mat_hbm, mat.at[pl.ds(2, tile_x)], in_sem.at[0])]
    for c, src in enumerate(STRESS_FROM):
        loads.append(
            pltpu.make_async_copy(
                rec_hbm.at[0, :, 3 + src], stress.at[:, c, pl.ds(2, tile_x)], in_sem.at[1 + c]
            )
        )
    for c in range(3):
        loads.append(
            pltpu.make_async_copy(
                rec_hbm.at[0, :, c], vel.at[1, :, c, pl.ds(4, tile_x)], in_sem.at[7 + c]
            )
        )
    own_rows = pltpu.make_async_copy(
        src_hbm.at[0, :, :, pl.ds(2 * sx, 2)], rows_in.at[sx], in_sem.at[10]
    )
    smalls = (
        (table_hbm, table_ref),
        (res_hbm, res_ref),
        (cell_hbm, cell_ref),
        (listed_hbm, listed_ref),
        (pick_hbm, pick_ref),
    )
    for k, (a, b) in enumerate(smalls):
        loads.insert(1 + k, pltpu.make_async_copy(a, b, in_sem.at[11 + k]))
    for load in loads:
        load.start()
    own_rows.start()

    zero = jnp.zeros((rows, depth), F32)
    none = jnp.full((rows, depth), -1, jnp.int32)
    for row in (0, 1, tile_x + 2, tile_x + 3):
        mat[row] = none
    for row in range(tile_x):
        mat_y[row] = none

    @pl.loop(0, recs)
    def _(r):
        for c in range(6):
            for row in (0, 1, tile_x + 2, tile_x + 3):
                stress[r, c, row] = zero
        for c in range(3):
            for row in range(tile_x):
                stress_y[r, c, row] = zero
            for p in range(2):
                for row in range(4):
                    vel[p, r, c, row] = zero
                    vel[p, r, c, tile_x + 4 + row] = zero
                for row in range(tile_x + 4):
                    vel_y[p, r, c, row] = zero
                for side in range(2):
                    for k in range(FAR):
                        far_in[p, r, side, c, k] = zero.astype(BF16)

    barrier = pltpu.get_barrier_semaphore()

    def has(way):
        dx, dy = WAYS[way]
        ok = None
        for d, at, count in ((dx, gx, n_gx), (dy, gy, n_gy)):
            if d:
                one = at > 0 if d < 0 else at < count - 1
                ok = one if ok is None else ok & one
        return ok

    def device(way):
        dx, dy = WAYS[way]
        return {"gx": jnp.clip(gx + dx, 0, n_gx - 1), "gy": jnp.clip(gy + dy, 0, n_gy - 1)}

    column = [2 * ((sx + d) % n_col) + sy for d in range(1, n_col)] + [2 * sx + 1 - sy]
    for to in column:
        pl.semaphore_signal(barrier, inc=1, device_id={"sta": to}, device_id_type=MESH)
    peers = len(column)
    for way in range(8):

        @pl.when(has(way))
        def _(way=way):
            pl.semaphore_signal(barrier, inc=1, device_id=device(way), device_id_type=MESH)

        peers = peers + has(way).astype(jnp.int32)

    @pl.loop(0, steps)
    def _(n):
        for c in range(6):
            for x in range(tile_x):
                weighted[n, c, x] = zero

    for load in loads:
        load.wait()
    pl.semaphore_wait(barrier, peers)

    def part(d, low, high):
        return low if d < 0 else high

    def mat_copy(way):
        dx, dy = WAYS[way]
        if dx:
            src = mat.at[pl.ds(part(dx, 2, tile_x), 2)]
            dst = mat.at[pl.ds(part(dx, tile_x + 2, 0), 2)]
        else:
            at_row = pl.ds(part(dy, 0, rows - 2), 2)
            src, dst = mat.at[pl.ds(2, tile_x), at_row], mat_y.at[:, at_row]
        return pltpu.make_async_remote_copy(
            src_ref=src,
            dst_ref=dst,
            send_sem=m_send.at[way],
            recv_sem=m_recv.at[way],
            device_id=device(way),
            device_id_type=MESH,
        )

    def stress_copy(way, r):
        dx, dy = WAYS[way]
        if dx:
            src = stress.at[r, pl.ds(XY, 3), pl.ds(part(dx, 2, tile_x), 2)]
            dst = stress.at[r, pl.ds(XY, 3), pl.ds(part(dx, tile_x + 2, 0), 2)]
        else:
            at_row = pl.ds(part(dy, 0, rows - 2), 2)
            src = stress.at[r, pl.ds(0, 3), pl.ds(2, tile_x), at_row]
            dst = stress_y.at[r, :, :, at_row]
        return pltpu.make_async_remote_copy(
            src_ref=src,
            dst_ref=dst,
            send_sem=i_send.at[way, r],
            recv_sem=i_recv.at[way, r],
            device_id=device(way),
            device_id_type=MESH,
        )

    def vel_copy(way, p, r):
        dx, dy = WAYS[way]
        if dx and dy:
            at_row = pl.ds(part(dy, 0, rows - 2), 2)
            src = vel.at[p, r, pl.ds(0, 2), pl.ds(part(dx, 4, tile_x + 2), 2), at_row]
            dst = vel_y.at[p, r, pl.ds(0, 2), pl.ds(part(dx, tile_x + 2, 0), 2), at_row]
        elif way >= 8:
            src = far_out.at[p, r, way - 8]
            dst = far_in.at[p, r, way - 8]
        elif dx:
            src = vel.at[p, r, :, pl.ds(part(dx, 4, tile_x + 2), 2)]
            dst = vel.at[p, r, :, pl.ds(part(dx, tile_x + 4, 2), 2)]
        else:
            at_row = pl.ds(part(dy, 0, rows - 4), 4)
            src = vel.at[p, r, :, pl.ds(4, tile_x), at_row]
            dst = vel_y.at[p, r, :, pl.ds(2, tile_x), at_row]
        return pltpu.make_async_remote_copy(
            src_ref=src,
            dst_ref=dst,
            send_sem=h_send.at[p, way, r],
            recv_sem=h_recv.at[p, way, r],
            device_id=device(way),
            device_id_type=MESH,
        )

    def send(copy, ways, *at):
        for way in ways:

            @pl.when(has(way))
            def _(way=way):
                copy(way, *at).start()

    def arrive(copy, ways, *at):
        for way in ways:

            @pl.when(has(BACK[way]))
            def _(way=way):
                copy(way, *at).wait_recv()

            @pl.when(has(way))
            def _(way=way):
                copy(way, *at).wait_send()

    edges, corners, all_ways = (8, 9, 0, 1, 2, 3), range(4, 8), (8, 9, *range(8))
    sides = range(4)

    @pl.loop(0, recs)
    def _(r):
        send(stress_copy, sides, r)

    send(mat_copy, sides)

    def row_copy(d):
        to = (sx + d) % n_col
        return pltpu.make_async_remote_copy(
            src_ref=src_hbm.at[0, :, :, pl.ds(2 * to, 2)],
            dst_ref=rows_in.at[sx],
            send_sem=a_send.at[d - 1],
            recv_sem=a_recv.at[d - 1],
            device_id={"sta": 2 * to + sy},
            device_id_type=MESH,
        )

    for d in range(1, n_col):
        row_copy(d).start()

    def piece(q):
        return pltpu.make_async_remote_copy(
            src_ref=mine.at[q],
            dst_ref=other.at[q],
            send_sem=b_send.at[q],
            recv_sem=b_recv.at[q],
            device_id={"sta": 2 * sx + 1 - sy},
            device_id_type=MESH,
        )

    def ring(k, t):
        step = 1 if k % 2 == 0 else n_col - 1
        to = (sx + step) % n_col
        slot = sx if k < 2 else (sx + n_col - step) % n_col
        half = steps // 2
        begin, size = (0, steps) if k < 2 else ((k - 2) * half, half)
        ref = gath.at[slot, pl.ds(t * steps + begin, size)]
        return pltpu.make_async_remote_copy(
            src_ref=ref,
            dst_ref=ref,
            send_sem=g_send.at[k, t],
            recv_sem=g_recv.at[k, t],
            device_id={"sta": 2 * to + sy},
            device_id_type=MESH,
        )

    def take_rows():
        own_rows.wait()
        for d in range(1, n_col):
            row_copy(d).wait()

    def pick_piece(q):
        m = q % steps
        p = pick_ref[q // steps, m]
        keep = p % 2 == sy
        for c in range(6):
            for j in range(2):
                v = rows_in[p // 2, m, c, j]
                mine[q, c, j] = jnp.where(keep, v, jnp.zeros_like(v))
        piece(q).start()

    def gather_rows(t):
        @pl.loop(0, steps)
        def _(m):
            q = t * steps + m
            piece(q).wait()
            for c in range(6):
                for j in range(2):
                    gath[sx, q, c, j] = mine[q, c, j] + other[q, c, j]

        ring(0, t).start()
        ring(1, t).start()

    def relay_rows(t):
        for k in range(4):
            if k < 2:
                ring(k, t).wait()
            else:
                ring(k, t).start()

    row_at = lax.broadcasted_iota(jnp.int32, (rows, depth), 0)
    lane_at = lax.broadcasted_iota(jnp.int32, (rows, depth), 1)
    first1, first2 = row_at < 1, row_at < 2
    last1, last2 = row_at >= rows - 1, row_at >= rows - 2
    src_at = lax.broadcasted_iota(jnp.int32, (2 * depth, depth), 0) % depth
    off = src_at - lax.broadcasted_iota(jnp.int32, (2 * depth, depth), 1)
    band = jnp.where(off == 1, 1.0, 0.0) - jnp.where(off == -1, 1.0, 0.0)
    band = band + 0.125 * (jnp.where(off == -2, 1.0, 0.0) - jnp.where(off == 2, 1.0, 0.0))
    band = band.astype(BF16)

    def diff_x(get, c, x):
        return (get(c, x + 1) - get(c, x - 1)) - 0.125 * (get(c, x + 2) - get(c, x - 2))

    def diff_y(t, e):
        up1 = pltpu.roll(jnp.where(first1, e, t), rows - 1, 0)
        up2 = pltpu.roll(jnp.where(first2, e, t), rows - 2, 0)
        dn1 = pltpu.roll(jnp.where(last1, e, t), 1, 0)
        dn2 = pltpu.roll(jnp.where(last2, e, t), 2, 0)
        return (up1 - dn1) - 0.125 * (up2 - dn2)

    def diff_z(f):
        planes = f.shape[0]
        f = f.reshape(planes * rows, depth)
        hi = f.astype(BF16)
        lo = (f - hi.astype(F32)).astype(BF16)
        both = jnp.concatenate([hi, lo], 1)
        d = jnp.dot(both, band, preferred_element_type=F32)
        return d.reshape(planes, rows, depth)

    tile = range(tile_x)

    def tables():
        def look(m, k):
            v = jnp.zeros((rows, depth), F32)
            for j in range(table_ref.shape[1]):
                v = jnp.where(m == j, table_ref[k, j], v)
            return v

        unit = TIME_STEP * STIFFNESS * C_NEAR
        for x in range(tile_x + 4):
            for k in (1, 2):
                coef[k, x] = unit * look(mat[x], k)
        for x in tile:
            for k in (1, 2):
                coef_y[k - 1, x] = unit * look(mat_y[x], k)

    def buoyancy():
        for x in tile:
            m = mat[x + 2]
            v = jnp.ones((rows, depth), F32)
            for j in range(table_ref.shape[1]):
                v = jnp.where(m == j, table_ref[0, j], v)
            coef[0, x + 2] = TIME_STEP * C_NEAR / v

    def velocity(n, p, r):
        def s(c, x):
            return stress[r, c, x + 2]

        def e(c, x):
            return stress_y[r, c, x]

        zx, zy, zz = (diff_z(stress[r, c, pl.ds(2, tile_x)]) for c in (XZ, YZ, ZZ))
        cell = cell_ref[0, r]
        cx = cell // (n_gy * rows) - gx * tile_x
        cy = cell % (n_gy * rows) - gy * rows
        amp = (AMPLITUDE / C_NEAR) * res_ref[0, r, n]
        spot = jnp.where((row_at == cy) & (lane_at == 0), amp, 0.0)
        for x in tile:
            b = coef[0, x + 2]
            fx = diff_x(s, XX, x) + diff_y(s(XY, x), e(XY, x)) + zx[x]
            fy = diff_x(s, XY, x) + diff_y(s(YY, x), e(YY, x)) + zy[x]
            fz = diff_x(s, XZ, x) + diff_y(s(YZ, x), e(YZ, x)) + zz[x]
            fz = fz + spot * jnp.where(cx == x, 1.0, 0.0)
            for c, f in ((VX, fx), (VY, fy), (VZ, fz)):
                vel[p, r, c, x + 4] = vel[1 - p, r, c, x + 4] + b * f
        for c in range(3):
            for side, (first, way) in enumerate(((6, 1), (tile_x + 1, -1))):
                for k in range(FAR):
                    far_out[p, r, side, c, k] = vel[p, r, c, first + way * k].astype(BF16)

    def unpack(p, r):
        for c in range(3):
            for side, (first, way) in enumerate(((tile_x + 6, 1), (1, -1))):
                for k in range(FAR):
                    vel[p, r, c, first + way * k] = far_in[p, r, side, c, k].astype(F32)

    def strain(n, p, r):
        def v(c, x):
            return vel[p, r, c, x + 4]

        def e(c, x):
            return vel_y[p, r, c, x + 2]

        zx, zy, zz = (diff_z(vel[p, r, c, pl.ds(4, tile_x)]) for c in (VX, VY, VZ))
        res = res_ref[0, r, n]
        for x in tile:
            la, mu = coef[1, x + 2], coef[2, x + 2]
            mu2 = mu + mu
            rxx = diff_x(v, VX, x)
            ryy = diff_y(v(VY, x), e(VY, x))
            rzz = zz[x]
            rxy = diff_y(v(VX, x), e(VX, x)) + diff_x(v, VY, x)
            rxz = zx[x] + diff_x(v, VZ, x)
            ryz = zy[x] + diff_y(v(VZ, x), e(VZ, x))
            tr = la * (rxx + ryy + rzz)
            put = ((XX, rxx), (YY, ryy), (ZZ, rzz), (XY, rxy), (XZ, rxz), (YZ, ryz))
            for k, (c, d) in enumerate(put):
                weighted[n, k, x] = weighted[n, k, x] + res * d
                step = tr + mu2 * d if k < 3 else mu * d
                stress[r, c, x + 2] = stress[r, c, x + 2] + step

    def strain_edges(p, r):
        def v(c, x):
            return vel[p, r, c, x + 4]

        def e(c, x):
            return vel_y[p, r, c, x + 2]

        for low in (-2, tile_x):
            zx, zz = (diff_z(vel[p, r, c, pl.ds(low + 4, 2)]) for c in (VX, VZ))
            for k in range(2):
                x = low + k
                la, mu = coef[1, x + 2], coef[2, x + 2]
                rxx = diff_x(v, VX, x)
                ryy = diff_y(v(VY, x), e(VY, x))
                rxy = diff_y(v(VX, x), e(VX, x)) + diff_x(v, VY, x)
                rxz = zx[k] + diff_x(v, VZ, x)
                sxx = la * (rxx + ryy + zz[k]) + (mu + mu) * rxx
                for c, step in ((XX, sxx), (XY, mu * rxy), (XZ, mu * rxz)):
                    stress[r, c, x + 2] = stress[r, c, x + 2] + step
        zy, zz = (diff_z(vel_y[p, r, c, pl.ds(2, tile_x)]) for c in (VY, VZ))
        for x in tile:
            la, mu = coef_y[0, x], coef_y[1, x]
            rxx = diff_x(e, VX, x)
            ryy = diff_y(e(VY, x), v(VY, x))
            rxy = diff_y(e(VX, x), v(VX, x)) + diff_x(e, VY, x)
            ryz = zy[x] + diff_y(e(VZ, x), v(VZ, x))
            syy = la * (rxx + ryy + zz[x]) + (mu + mu) * ryy
            for c, step in ((YY, syy), (XY, mu * rxy), (YZ, mu * ryz)):
                stress_y[r, c, x] = stress_y[r, c, x] + step

    buoyancy()
    first_piece = 2

    @pl.loop(0, recs)
    def _(r):
        arrive(stress_copy, sides, r)
        velocity(0, 0, r)
        send(vel_copy, all_ways, 0, r)

    arrive(mat_copy, sides)
    tables()

    @pl.loop(0, steps)
    def _(n):
        p = n % 2
        pl.when(n == first_piece)(take_rows)

        @pl.loop(0, recs)
        def _(r):
            arrive(vel_copy, edges, p, r)
            unpack(p, r)
            strain(n, p, r)
            arrive(vel_copy, corners, p, r)

            @pl.when(n < steps - 1)
            def _():
                strain_edges(p, r)
                velocity(n + 1, 1 - p, r)
                send(vel_copy, all_ways, 1 - p, r)

            @pl.when((n >= first_piece) & (n < first_piece + turns))
            def _():
                for j in range(steps // recs):
                    pick_piece((n - first_piece) * steps + r * (steps // recs) + j)

        for t in range(turns):
            pl.when(n == first_piece + 1 + t)(functools.partial(gather_rows, t))
            pl.when(n == first_piece + 3 + t)(functools.partial(relay_rows, t))

    for t in range(turns):
        ring(2, t).wait()
        ring(3, t).wait()

    for x in range(tile_x):
        for k in range(2):
            acc[x, k] = zero

    scale = KERNEL_SCALE * C_NEAR

    @pl.loop(0, steps)
    def _(n):
        share = [listed_ref[t, n, sta].astype(F32) for t in range(turns)]
        for x in range(tile_x):
            comb = []
            for c in range(6):
                total = None
                for t in range(turns):
                    v = share[t] * gath[x // 2, t * steps + n, c, x % 2].astype(F32)
                    total = v if total is None else total + v
                comb.append(total)
            w = [weighted[n, k, x] for k in range(6)]
            lam = (comb[0] + comb[1] + comb[2]) * (w[0] + w[1] + w[2])
            mu = comb[0] * w[0]
            for c in range(1, 6):
                mu = mu + comb[c] * w[c]
            acc[x, 0] = acc[x, 0] + scale * lam
            acc[x, 1] = acc[x, 1] + (2.0 * scale) * mu

    def share_copy(d):
        to = (sta + d) % n_sta
        return pltpu.make_async_remote_copy(
            src_ref=acc.at[to],
            dst_ref=parts.at[d],
            send_sem=r_send.at[d],
            recv_sem=r_recv.at[d],
            device_id={"sta": to},
            device_id_type=MESH,
        )

    for d in range(1, n_sta):
        share_copy(d).start()
    for k in range(2):
        out_ref[k, 0] = acc[sta, k]
    for d in range(1, n_sta):
        share_copy(d).wait()
        for k in range(2):
            out_ref[k, 0] = out_ref[k, 0] + parts[d, k]


def local(rec_state, source_strain, material, material_table, residual, rec_cell, listed, src_pick):
    _, recs, _, tile_x, tile_y, depth = rec_state.shape
    steps = source_strain.shape[1]
    turns = listed.shape[0]
    n_sta = lax.axis_size("sta")
    n_col = n_sta // 2
    plane = (tile_y, depth)
    hbm = pl.BlockSpec(memory_space=pltpu.HBM)
    table = material_table.T
    smalls = (table, residual, rec_cell, listed, src_pick)
    dma = pltpu.SemaphoreType.DMA
    return pl.pallas_call(
        body,
        out_shape=jax.ShapeDtypeStruct((2, 1, *plane), F32),
        in_specs=[hbm] * 8,
        out_specs=pl.BlockSpec(memory_space=pltpu.VMEM),
        scratch_shapes=[
            pltpu.VMEM((recs, 6, tile_x + 4, *plane), F32),
            pltpu.VMEM((recs, 3, tile_x, *plane), F32),
            pltpu.VMEM((2, recs, 3, tile_x + 8, *plane), F32),
            pltpu.VMEM((2, recs, 3, tile_x + 4, *plane), F32),
            pltpu.VMEM((2, recs, 2, 3, FAR, *plane), BF16),
            pltpu.VMEM((2, recs, 2, 3, FAR, *plane), BF16),
            pltpu.VMEM((steps, 6, tile_x, *plane), F32),
            pltpu.VMEM((tile_x + 4, *plane), jnp.int32),
            pltpu.VMEM((tile_x, *plane), jnp.int32),
            pltpu.VMEM((3, tile_x + 4, *plane), F32),
            pltpu.VMEM((2, tile_x, *plane), F32),
            pltpu.VMEM((n_col, steps, 6, 2, *plane), BF16),
            pltpu.VMEM((turns * steps, 6, 2, *plane), BF16),
            pltpu.VMEM((turns * steps, 6, 2, *plane), BF16),
            pltpu.VMEM((n_col, turns * steps, 6, 2, *plane), BF16),
            pltpu.VMEM((tile_x, 2, *plane), F32),
            pltpu.VMEM((n_sta, 2, *plane), F32),
            *[pltpu.SMEM(a.shape, a.dtype) for a in smalls],
            dma((16,)),
            dma((4,)),
            dma((4,)),
            dma((4, recs)),
            dma((4, recs)),
            dma((2, 10, recs)),
            dma((2, 10, recs)),
            dma((n_col - 1,)),
            dma((n_col - 1,)),
            dma((turns * steps,)),
            dma((turns * steps,)),
            dma((4, turns)),
            dma((4, turns)),
            dma((n_sta,)),
            dma((n_sta,)),
        ],
        compiler_params=pltpu.CompilerParams(
            collective_id=0, has_side_effects=True
        ),
        name="kernels",
    )(rec_state, source_strain, material, *smalls)


def solution(mesh):
    in_specs = (
        P("sta", None, None, "gx", "gy", None),
        P("sta", None, None, "gx", "gy", None),
        P("gx", "gy", None),
        P(),
        P("sta", None, None),
        P("sta", None),
        P(),
        P(),
    )
    out_specs = P(None, ("gx", "sta"), "gy", None)
    return jax.shard_map(local, mesh=mesh, in_specs=in_specs, out_specs=out_specs, check_vma=False)
```

```python
import functools

import jax
import jax.numpy as jnp
from jax import lax
from jax.experimental import pallas as pl
from jax.experimental.pallas import tpu as pltpu
from jax.sharding import PartitionSpec as P

MESH = pl.DeviceIdType.MESH
F32 = jnp.float32
BF16 = jnp.bfloat16

C_NEAR = 8.0 / 12.0
TIME_STEP = 0.25
AMPLITUDE = 4.0
KERNEL_SCALE = 0.0625
STIFFNESS = 0.3

YY, YZ, XY, XX, XZ, ZZ = range(6)
STRESS_FROM = (1, 5, 3, 0, 4, 2)
VX, VY, VZ = range(3)
WAYS = ((-1, 0), (1, 0), (0, -1), (0, 1), (-1, -1), (-1, 1), (1, -1), (1, 1), (-1, 0), (1, 0))
BACK = (1, 0, 3, 2, 7, 6, 5, 4, 9, 8)
FAR = 2


def body(
    rec_hbm,
    src_hbm,
    mat_hbm,
    table_hbm,
    res_hbm,
    cell_hbm,
    listed_hbm,
    pick_hbm,
    out_ref,
    stress,
    stress_y,
    vel,
    vel_y,
    far_out,
    far_in,
    weighted,
    mat,
    mat_y,
    coef,
    coef_y,
    rows_in,
    mine,
    other,
    gath,
    acc,
    parts,
    table_ref,
    res_ref,
    cell_ref,
    listed_ref,
    pick_ref,
    in_sem,
    m_send,
    m_recv,
    i_send,
    i_recv,
    h_send,
    h_recv,
    a_send,
    a_recv,
    b_send,
    b_recv,
    g_send,
    g_recv,
    r_send,
    r_recv,
):
    recs = stress.shape[0]
    steps = weighted.shape[0]
    tile_x, rows, depth = coef_y.shape[1:]
    turns = listed_ref.shape[0]
    n_sta = parts.shape[0]
    n_col = gath.shape[0]
    gx, gy, sta = lax.axis_index("gx"), lax.axis_index("gy"), lax.axis_index("sta")
    n_gx, n_gy = lax.axis_size("gx"), lax.axis_size("gy")
    sx, sy = sta // 2, sta % 2

    loads = [pltpu.make_async_copy(mat_hbm, mat.at[pl.ds(2, tile_x)], in_sem.at[0])]
    for c, src in enumerate(STRESS_FROM):
        loads.append(
            pltpu.make_async_copy(
                rec_hbm.at[0, :, 3 + src], stress.at[:, c, pl.ds(2, tile_x)], in_sem.at[1 + c]
            )
        )
    for c in range(3):
        loads.append(
            pltpu.make_async_copy(
                rec_hbm.at[0, :, c], vel.at[1, :, c, pl.ds(4, tile_x)], in_sem.at[7 + c]
            )
        )
    own_rows = pltpu.make_async_copy(
        src_hbm.at[0, :, :, pl.ds(2 * sx, 2)], rows_in.at[sx], in_sem.at[10]
    )
    smalls = (
        (table_hbm, table_ref),
        (res_hbm, res_ref),
        (cell_hbm, cell_ref),
        (listed_hbm, listed_ref),
        (pick_hbm, pick_ref),
    )
    for k, (a, b) in enumerate(smalls):
        loads.insert(1 + k, pltpu.make_async_copy(a, b, in_sem.at[11 + k]))
    for load in loads:
        load.start()
    own_rows.start()

    zero = jnp.zeros((rows, depth), F32)
    none = jnp.full((rows, depth), -1, jnp.int32)
    for row in (0, 1, tile_x + 2, tile_x + 3):
        mat[row] = none
    for row in range(tile_x):
        mat_y[row] = none

    @pl.loop(0, recs)
    def _(r):
        for c in range(6):
            for row in (0, 1, tile_x + 2, tile_x + 3):
                stress[r, c, row] = zero
        for c in range(3):
            for row in range(tile_x):
                stress_y[r, c, row] = zero
            for p in range(2):
                for row in range(4):
                    vel[p, r, c, row] = zero
                    vel[p, r, c, tile_x + 4 + row] = zero
                for row in range(tile_x + 4):
                    vel_y[p, r, c, row] = zero
                for side in range(2):
                    for k in range(FAR):
                        far_in[p, r, side, c, k] = zero.astype(BF16)

    barrier = pltpu.get_barrier_semaphore()

    def has(way):
        dx, dy = WAYS[way]
        ok = None
        for d, at, count in ((dx, gx, n_gx), (dy, gy, n_gy)):
            if d:
                one = at > 0 if d < 0 else at < count - 1
                ok = one if ok is None else ok & one
        return ok

    def device(way):
        dx, dy = WAYS[way]
        return {"gx": jnp.clip(gx + dx, 0, n_gx - 1), "gy": jnp.clip(gy + dy, 0, n_gy - 1)}

    column = [2 * ((sx + d) % n_col) + sy for d in range(1, n_col)] + [2 * sx + 1 - sy]
    for to in column:
        pl.semaphore_signal(barrier, inc=1, device_id={"sta": to}, device_id_type=MESH)
    peers = len(column)
    for way in range(8):

        @pl.when(has(way))
        def _(way=way):
            pl.semaphore_signal(barrier, inc=1, device_id=device(way), device_id_type=MESH)

        peers = peers + has(way).astype(jnp.int32)

    @pl.loop(0, steps)
    def _(n):
        for c in range(6):
            for x in range(tile_x):
                weighted[n, c, x] = zero

    for load in loads:
        load.wait()
    pl.semaphore_wait(barrier, peers)

    def part(d, low, high):
        return low if d < 0 else high

    def mat_copy(way):
        dx, dy = WAYS[way]
        if dx:
            src = mat.at[pl.ds(part(dx, 2, tile_x), 2)]
            dst = mat.at[pl.ds(part(dx, tile_x + 2, 0), 2)]
        else:
            at_row = pl.ds(part(dy, 0, rows - 2), 2)
            src, dst = mat.at[pl.ds(2, tile_x), at_row], mat_y.at[:, at_row]
        return pltpu.make_async_remote_copy(
            src_ref=src,
            dst_ref=dst,
            send_sem=m_send.at[way],
            recv_sem=m_recv.at[way],
            device_id=device(way),
            device_id_type=MESH,
        )

    def stress_copy(way, r):
        dx, dy = WAYS[way]
        if dx:
            src = stress.at[r, pl.ds(XY, 3), pl.ds(part(dx, 2, tile_x), 2)]
            dst = stress.at[r, pl.ds(XY, 3), pl.ds(part(dx, tile_x + 2, 0), 2)]
        else:
            at_row = pl.ds(part(dy, 0, rows - 2), 2)
            src = stress.at[r, pl.ds(0, 3), pl.ds(2, tile_x), at_row]
            dst = stress_y.at[r, :, :, at_row]
        return pltpu.make_async_remote_copy(
            src_ref=src,
            dst_ref=dst,
            send_sem=i_send.at[way, r],
            recv_sem=i_recv.at[way, r],
            device_id=device(way),
            device_id_type=MESH,
        )

    def vel_copy(way, p, r):
        dx, dy = WAYS[way]
        if dx and dy:
            at_row = pl.ds(part(dy, 0, rows - 2), 2)
            src = vel.at[p, r, pl.ds(0, 2), pl.ds(part(dx, 4, tile_x + 2), 2), at_row]
            dst = vel_y.at[p, r, pl.ds(0, 2), pl.ds(part(dx, tile_x + 2, 0), 2), at_row]
        elif way >= 8:
            src = far_out.at[p, r, way - 8]
            dst = far_in.at[p, r, way - 8]
        elif dx:
            src = vel.at[p, r, :, pl.ds(part(dx, 4, tile_x + 2), 2)]
            dst = vel.at[p, r, :, pl.ds(part(dx, tile_x + 4, 2), 2)]
        else:
            at_row = pl.ds(part(dy, 0, rows - 4), 4)
            src = vel.at[p, r, :, pl.ds(4, tile_x), at_row]
            dst = vel_y.at[p, r, :, pl.ds(2, tile_x), at_row]
        return pltpu.make_async_remote_copy(
            src_ref=src,
            dst_ref=dst,
            send_sem=h_send.at[p, way, r],
            recv_sem=h_recv.at[p, way, r],
            device_id=device(way),
            device_id_type=MESH,
        )

    def send(copy, ways, *at):
        for way in ways:

            @pl.when(has(way))
            def _(way=way):
                copy(way, *at).start()

    def arrive(copy, ways, *at):
        for way in ways:

            @pl.when(has(BACK[way]))
            def _(way=way):
                copy(way, *at).wait_recv()

            @pl.when(has(way))
            def _(way=way):
                copy(way, *at).wait_send()

    sides, outer, all_ways = range(4), (8, 9, 4, 5, 6, 7), (4, 5, 6, 7, 0, 1, 2, 3, 8, 9)

    @pl.loop(0, recs)
    def _(r):
        send(stress_copy, sides, r)

    send(mat_copy, sides)

    def row_copy(d):
        to = (sx + d) % n_col
        return pltpu.make_async_remote_copy(
            src_ref=src_hbm.at[0, :, :, pl.ds(2 * to, 2)],
            dst_ref=rows_in.at[sx],
            send_sem=a_send.at[d - 1],
            recv_sem=a_recv.at[d - 1],
            device_id={"sta": 2 * to + sy},
            device_id_type=MESH,
        )

    for d in range(1, n_col):
        row_copy(d).start()

    def piece(q):
        return pltpu.make_async_remote_copy(
            src_ref=mine.at[q],
            dst_ref=other.at[q],
            send_sem=b_send.at[q],
            recv_sem=b_recv.at[q],
            device_id={"sta": 2 * sx + 1 - sy},
            device_id_type=MESH,
        )

    chunk = 4

    def ring(k, t):
        step = 1 if k % 2 == 0 else n_col - 1
        to = (sx + step) % n_col
        slot = sx if k < 2 else (sx + n_col - step) % n_col
        half = chunk // 2
        begin, size = (0, chunk) if k < 2 else ((k - 2) * half, half)
        ref = gath.at[slot, pl.ds(t * chunk + begin, size)]
        return pltpu.make_async_remote_copy(
            src_ref=ref,
            dst_ref=ref,
            send_sem=g_send.at[k, t],
            recv_sem=g_recv.at[k, t],
            device_id={"sta": 2 * to + sy},
            device_id_type=MESH,
        )

    def take_rows():
        own_rows.wait()
        for d in range(1, n_col):
            row_copy(d).wait()

    def pick_piece(q):
        m = q % steps
        p = pick_ref[q // steps, m]
        keep = p % 2 == sy
        for c in range(6):
            for j in range(2):
                v = rows_in[p // 2, m, c, j]
                mine[q, c, j] = jnp.where(keep, v, jnp.zeros_like(v))
        piece(q).start()

    def gather_rows(t):
        @pl.loop(t * chunk, (t + 1) * chunk)
        def _(q):
            piece(q).wait()
            for c in range(6):
                for j in range(2):
                    gath[sx, q, c, j] = mine[q, c, j] + other[q, c, j]

        ring(0, t).start()
        ring(1, t).start()

    def relay_rows(t):
        for k in range(4):
            if k < 2:
                ring(k, t).wait()
            else:
                ring(k, t).start()

    row_at = lax.broadcasted_iota(jnp.int32, (rows, depth), 0)
    lane_at = lax.broadcasted_iota(jnp.int32, (rows, depth), 1)
    first1, first2 = row_at < 1, row_at < 2
    last1, last2 = row_at >= rows - 1, row_at >= rows - 2
    src_at = lax.broadcasted_iota(jnp.int32, (2 * depth, depth), 0) % depth
    off = src_at - lax.broadcasted_iota(jnp.int32, (2 * depth, depth), 1)
    band = jnp.where(off == 1, 1.0, 0.0) - jnp.where(off == -1, 1.0, 0.0)
    band = band + 0.125 * (jnp.where(off == -2, 1.0, 0.0) - jnp.where(off == 2, 1.0, 0.0))
    band = band.astype(BF16)

    def diff_x(get, c, x):
        return (get(c, x + 1) - get(c, x - 1)) - 0.125 * (get(c, x + 2) - get(c, x - 2))

    def diff_y(t, e):
        up1 = pltpu.roll(jnp.where(first1, e, t), rows - 1, 0)
        up2 = pltpu.roll(jnp.where(first2, e, t), rows - 2, 0)
        dn1 = pltpu.roll(jnp.where(last1, e, t), 1, 0)
        dn2 = pltpu.roll(jnp.where(last2, e, t), 2, 0)
        return (up1 - dn1) - 0.125 * (up2 - dn2)

    def diff_z(f):
        planes = f.shape[0]
        f = f.reshape(planes * rows, depth)
        hi = f.astype(BF16)
        lo = (f - hi.astype(F32)).astype(BF16)
        both = jnp.concatenate([hi, lo], 1)
        d = jnp.dot(both, band, preferred_element_type=F32)
        return d.reshape(planes, rows, depth)

    tile = range(tile_x)

    def tables():
        def look(m, k):
            v = jnp.zeros((rows, depth), F32)
            for j in range(table_ref.shape[1]):
                v = jnp.where(m == j, table_ref[k, j], v)
            return v

        unit = TIME_STEP * STIFFNESS * C_NEAR
        for x in range(tile_x + 4):
            for k in (1, 2):
                coef[k, x] = unit * look(mat[x], k)
        for x in tile:
            for k in (1, 2):
                coef_y[k - 1, x] = unit * look(mat_y[x], k)

    def buoyancy():
        for x in tile:
            m = mat[x + 2]
            v = jnp.ones((rows, depth), F32)
            for j in range(table_ref.shape[1]):
                v = jnp.where(m == j, table_ref[0, j], v)
            coef[0, x + 2] = TIME_STEP * C_NEAR / v

    def velocity(n, p, r):
        def s(c, x):
            return stress[r, c, x + 2]

        def e(c, x):
            return stress_y[r, c, x]

        zx, zy, zz = (diff_z(stress[r, c, pl.ds(2, tile_x)]) for c in (XZ, YZ, ZZ))
        cell = cell_ref[0, r]
        cx = cell // (n_gy * rows) - gx * tile_x
        cy = cell % (n_gy * rows) - gy * rows
        amp = (AMPLITUDE / C_NEAR) * res_ref[0, r, n]
        spot = jnp.where((row_at == cy) & (lane_at == 0), amp, 0.0)
        for x in tile:
            b = coef[0, x + 2]
            fx = diff_x(s, XX, x) + diff_y(s(XY, x), e(XY, x)) + zx[x]
            fy = diff_x(s, XY, x) + diff_y(s(YY, x), e(YY, x)) + zy[x]
            fz = diff_x(s, XZ, x) + diff_y(s(YZ, x), e(YZ, x)) + zz[x]
            fz = fz + spot * jnp.where(cx == x, 1.0, 0.0)
            for c, f in ((VX, fx), (VY, fy), (VZ, fz)):
                vel[p, r, c, x + 4] = vel[1 - p, r, c, x + 4] + b * f
        for c in range(3):
            for side, (first, way) in enumerate(((6, 1), (tile_x + 1, -1))):
                for k in range(FAR):
                    far_out[p, r, side, c, k] = vel[p, r, c, first + way * k].astype(BF16)

    def unpack(p, r):
        for c in range(3):
            for side, (first, way) in enumerate(((tile_x + 6, 1), (1, -1))):
                for k in range(FAR):
                    vel[p, r, c, first + way * k] = far_in[p, r, side, c, k].astype(F32)

    def strain(n, p, r):
        def v(c, x):
            return vel[p, r, c, x + 4]

        def e(c, x):
            return vel_y[p, r, c, x + 2]

        zx, zy, zz = (diff_z(vel[p, r, c, pl.ds(4, tile_x)]) for c in (VX, VY, VZ))
        res = res_ref[0, r, n]
        for x in tile:
            la, mu = coef[1, x + 2], coef[2, x + 2]
            mu2 = mu + mu
            rxx = diff_x(v, VX, x)
            ryy = diff_y(v(VY, x), e(VY, x))
            rzz = zz[x]
            rxy = diff_y(v(VX, x), e(VX, x)) + diff_x(v, VY, x)
            rxz = zx[x] + diff_x(v, VZ, x)
            ryz = zy[x] + diff_y(v(VZ, x), e(VZ, x))
            tr = la * (rxx + ryy + rzz)
            put = ((XX, rxx), (YY, ryy), (ZZ, rzz), (XY, rxy), (XZ, rxz), (YZ, ryz))
            for k, (c, d) in enumerate(put):
                weighted[n, k, x] = weighted[n, k, x] + res * d
                step = tr + mu2 * d if k < 3 else mu * d
                stress[r, c, x + 2] = stress[r, c, x + 2] + step

    def strain_edges(p, r):
        def v(c, x):
            return vel[p, r, c, x + 4]

        def e(c, x):
            return vel_y[p, r, c, x + 2]

        for low in (-2, tile_x):
            zx, zz = (diff_z(vel[p, r, c, pl.ds(low + 4, 2)]) for c in (VX, VZ))
            for k in range(2):
                x = low + k
                la, mu = coef[1, x + 2], coef[2, x + 2]
                rxx = diff_x(v, VX, x)
                ryy = diff_y(v(VY, x), e(VY, x))
                rxy = diff_y(v(VX, x), e(VX, x)) + diff_x(v, VY, x)
                rxz = zx[k] + diff_x(v, VZ, x)
                sxx = la * (rxx + ryy + zz[k]) + (mu + mu) * rxx
                for c, step in ((XX, sxx), (XY, mu * rxy), (XZ, mu * rxz)):
                    stress[r, c, x + 2] = stress[r, c, x + 2] + step
        zy, zz = (diff_z(vel_y[p, r, c, pl.ds(2, tile_x)]) for c in (VY, VZ))
        for x in tile:
            la, mu = coef_y[0, x], coef_y[1, x]
            rxx = diff_x(e, VX, x)
            ryy = diff_y(e(VY, x), v(VY, x))
            rxy = diff_y(e(VX, x), v(VX, x)) + diff_x(e, VY, x)
            ryz = zy[x] + diff_y(e(VZ, x), v(VZ, x))
            syy = la * (rxx + ryy + zz[x]) + (mu + mu) * ryy
            for c, step in ((YY, syy), (XY, mu * rxy), (YZ, mu * ryz)):
                stress_y[r, c, x] = stress_y[r, c, x] + step

    buoyancy()
    chunks = turns * steps // chunk

    @pl.loop(0, recs)
    def _(r):
        arrive(stress_copy, sides, r)
        velocity(0, 0, r)
        send(vel_copy, all_ways, 0, r)

    arrive(mat_copy, sides)
    tables()

    @pl.loop(0, steps)
    def _(n):
        p = n % 2
        @pl.loop(0, recs)
        def _(r):
            arrive(vel_copy, sides, p, r)
            strain(n, p, r)
            arrive(vel_copy, outer, p, r)

            @pl.when(n < steps - 1)
            def _():
                unpack(p, r)
                strain_edges(p, r)
                velocity(n + 1, 1 - p, r)
                send(vel_copy, all_ways, 1 - p, r)

            for t in range(chunks):
                pl.when((n == t + 2) & (r == 1))(functools.partial(gather_rows, t))

        pl.when(n == 0)(take_rows)

        @pl.when(n < chunks)
        def _():
            for j in range(chunk):
                pick_piece(n * chunk + j)

        for t in range(chunks):
            pl.when(n == t + 3)(functools.partial(relay_rows, t))

    for t in range(chunks):
        ring(2, t).wait()
        ring(3, t).wait()

    for x in range(tile_x):
        for k in range(2):
            acc[x, k] = zero

    scale = KERNEL_SCALE * C_NEAR

    @pl.loop(0, steps)
    def _(n):
        share = [listed_ref[t, n, sta].astype(F32) for t in range(turns)]
        for x in range(tile_x):
            comb = []
            for c in range(6):
                total = None
                for t in range(turns):
                    v = share[t] * gath[x // 2, t * steps + n, c, x % 2].astype(F32)
                    total = v if total is None else total + v
                comb.append(total)
            w = [weighted[n, k, x] for k in range(6)]
            lam = (comb[0] + comb[1] + comb[2]) * (w[0] + w[1] + w[2])
            mu = comb[0] * w[0]
            for c in range(1, 6):
                mu = mu + comb[c] * w[c]
            acc[x, 0] = acc[x, 0] + scale * lam
            acc[x, 1] = acc[x, 1] + (2.0 * scale) * mu

    def share_copy(d):
        to = (sta + d) % n_sta
        return pltpu.make_async_remote_copy(
            src_ref=acc.at[to],
            dst_ref=parts.at[d],
            send_sem=r_send.at[d],
            recv_sem=r_recv.at[d],
            device_id={"sta": to},
            device_id_type=MESH,
        )

    for d in range(1, n_sta):
        share_copy(d).start()
    for k in range(2):
        out_ref[k, 0] = acc[sta, k]
    for d in range(1, n_sta):
        share_copy(d).wait()
        for k in range(2):
            out_ref[k, 0] = out_ref[k, 0] + parts[d, k]


def local(rec_state, source_strain, material, material_table, residual, rec_cell, listed, src_pick):
    _, recs, _, tile_x, tile_y, depth = rec_state.shape
    steps = source_strain.shape[1]
    turns = listed.shape[0]
    n_sta = lax.axis_size("sta")
    n_col = n_sta // 2
    plane = (tile_y, depth)
    hbm = pl.BlockSpec(memory_space=pltpu.HBM)
    table = material_table.T
    smalls = (table, residual, rec_cell, listed, src_pick)
    dma = pltpu.SemaphoreType.DMA
    return pl.pallas_call(
        body,
        out_shape=jax.ShapeDtypeStruct((2, 1, *plane), F32),
        in_specs=[hbm] * 8,
        out_specs=pl.BlockSpec(memory_space=pltpu.VMEM),
        scratch_shapes=[
            pltpu.VMEM((recs, 6, tile_x + 4, *plane), F32),
            pltpu.VMEM((recs, 3, tile_x, *plane), F32),
            pltpu.VMEM((2, recs, 3, tile_x + 8, *plane), F32),
            pltpu.VMEM((2, recs, 3, tile_x + 4, *plane), F32),
            pltpu.VMEM((2, recs, 2, 3, FAR, *plane), BF16),
            pltpu.VMEM((2, recs, 2, 3, FAR, *plane), BF16),
            pltpu.VMEM((steps, 6, tile_x, *plane), F32),
            pltpu.VMEM((tile_x + 4, *plane), jnp.int32),
            pltpu.VMEM((tile_x, *plane), jnp.int32),
            pltpu.VMEM((3, tile_x + 4, *plane), F32),
            pltpu.VMEM((2, tile_x, *plane), F32),
            pltpu.VMEM((n_col, steps, 6, 2, *plane), BF16),
            pltpu.VMEM((turns * steps, 6, 2, *plane), BF16),
            pltpu.VMEM((turns * steps, 6, 2, *plane), BF16),
            pltpu.VMEM((n_col, turns * steps, 6, 2, *plane), BF16),
            pltpu.VMEM((tile_x, 2, *plane), F32),
            pltpu.VMEM((n_sta, 2, *plane), F32),
            *[pltpu.SMEM(a.shape, a.dtype) for a in smalls],
            dma((16,)),
            dma((4,)),
            dma((4,)),
            dma((4, recs)),
            dma((4, recs)),
            dma((2, 10, recs)),
            dma((2, 10, recs)),
            dma((n_col - 1,)),
            dma((n_col - 1,)),
            dma((turns * steps,)),
            dma((turns * steps,)),
            dma((4, turns * steps // 4)),
            dma((4, turns * steps // 4)),
            dma((n_sta,)),
            dma((n_sta,)),
        ],
        compiler_params=pltpu.CompilerParams(
            collective_id=0, has_side_effects=True
        ),
        name="kernels",
    )(rec_state, source_strain, material, *smalls)


def solution(mesh):
    in_specs = (
        P("sta", None, None, "gx", "gy", None),
        P("sta", None, None, "gx", "gy", None),
        P("gx", "gy", None),
        P(),
        P("sta", None, None),
        P("sta", None),
        P(),
        P(),
    )
    out_specs = P(None, ("gx", "sta"), "gy", None)
    return jax.shard_map(local, mesh=mesh, in_specs=in_specs, out_specs=out_specs, check_vma=False)
```

```python
import functools

import jax
import jax.numpy as jnp
from jax import lax
from jax.experimental import pallas as pl
from jax.experimental.pallas import tpu as pltpu
from jax.sharding import PartitionSpec as P

MESH = pl.DeviceIdType.MESH
F32 = jnp.float32
BF16 = jnp.bfloat16

C_NEAR = 8.0 / 12.0
TIME_STEP = 0.25
AMPLITUDE = 4.0
KERNEL_SCALE = 0.0625
STIFFNESS = 0.3

YY, YZ, XY, XX, XZ, ZZ = range(6)
STRESS_FROM = (1, 5, 3, 0, 4, 2)
VX, VY, VZ = range(3)
WAYS = ((-1, 0), (1, 0), (0, -1), (0, 1), (-1, -1), (-1, 1), (1, -1), (1, 1), (-1, 0), (1, 0))
BACK = (1, 0, 3, 2, 7, 6, 5, 4, 9, 8)
FAR = 2


def body(
    rec_hbm,
    src_hbm,
    mat_hbm,
    table_hbm,
    res_hbm,
    cell_hbm,
    listed_hbm,
    pick_hbm,
    out_ref,
    stress,
    stress_y,
    vel,
    vel_y,
    far_out,
    far_in,
    cor_out,
    cor_in,
    weighted,
    mat,
    mat_y,
    coef,
    coef_y,
    rows_in,
    mine,
    other,
    gath,
    acc,
    parts,
    table_ref,
    res_ref,
    cell_ref,
    listed_ref,
    pick_ref,
    in_sem,
    m_send,
    m_recv,
    i_send,
    i_recv,
    h_send,
    h_recv,
    a_send,
    a_recv,
    b_send,
    b_recv,
    g_send,
    g_recv,
    r_send,
    r_recv,
):
    recs = stress.shape[0]
    steps = weighted.shape[0]
    tile_x, rows, depth = coef_y.shape[1:]
    turns = listed_ref.shape[0]
    n_sta = parts.shape[0]
    n_col = gath.shape[0]
    gx, gy, sta = lax.axis_index("gx"), lax.axis_index("gy"), lax.axis_index("sta")
    n_gx, n_gy = lax.axis_size("gx"), lax.axis_size("gy")
    sx, sy = sta // 2, sta % 2

    loads = [pltpu.make_async_copy(mat_hbm, mat.at[pl.ds(2, tile_x)], in_sem.at[0])]
    for c, src in enumerate(STRESS_FROM):
        loads.append(
            pltpu.make_async_copy(
                rec_hbm.at[0, :, 3 + src], stress.at[:, c, pl.ds(2, tile_x)], in_sem.at[1 + c]
            )
        )
    for c in range(3):
        loads.append(
            pltpu.make_async_copy(
                rec_hbm.at[0, :, c], vel.at[1, :, c, pl.ds(4, tile_x)], in_sem.at[7 + c]
            )
        )
    own_rows = pltpu.make_async_copy(
        src_hbm.at[0, :, :, pl.ds(2 * sx, 2)], rows_in.at[sx], in_sem.at[10]
    )
    smalls = (
        (table_hbm, table_ref),
        (res_hbm, res_ref),
        (cell_hbm, cell_ref),
        (listed_hbm, listed_ref),
        (pick_hbm, pick_ref),
    )
    for k, (a, b) in enumerate(smalls):
        loads.insert(1 + k, pltpu.make_async_copy(a, b, in_sem.at[11 + k]))
    for load in loads:
        load.start()
    own_rows.start()

    zero = jnp.zeros((rows, depth), F32)
    none = jnp.full((rows, depth), -1, jnp.int32)
    for row in (0, 1, tile_x + 2, tile_x + 3):
        mat[row] = none
    for row in range(tile_x):
        mat_y[row] = none

    @pl.loop(0, recs)
    def _(r):
        for p in range(2):
            for k in range(4):
                cor_in[p, r, k] = zero.astype(BF16)
        for c in range(6):
            for row in (0, 1, tile_x + 2, tile_x + 3):
                stress[r, c, row] = zero
        for c in range(3):
            for row in range(tile_x):
                stress_y[r, c, row] = zero
            for p in range(2):
                for row in range(4):
                    vel[p, r, c, row] = zero
                    vel[p, r, c, tile_x + 4 + row] = zero
                for row in range(tile_x + 4):
                    vel_y[p, r, c, row] = zero
                for side in range(2):
                    for k in range(FAR):
                        far_in[p, r, side, c, k] = zero.astype(BF16)

    barrier = pltpu.get_barrier_semaphore()

    def has(way):
        dx, dy = WAYS[way]
        ok = None
        for d, at, count in ((dx, gx, n_gx), (dy, gy, n_gy)):
            if d:
                one = at > 0 if d < 0 else at < count - 1
                ok = one if ok is None else ok & one
        return ok

    def device(way):
        dx, dy = WAYS[way]
        return {"gx": jnp.clip(gx + dx, 0, n_gx - 1), "gy": jnp.clip(gy + dy, 0, n_gy - 1)}

    column = [2 * ((sx + d) % n_col) + sy for d in range(1, n_col)] + [2 * sx + 1 - sy]
    for to in column:
        pl.semaphore_signal(barrier, inc=1, device_id={"sta": to}, device_id_type=MESH)
    peers = len(column)
    for way in range(8):

        @pl.when(has(way))
        def _(way=way):
            pl.semaphore_signal(barrier, inc=1, device_id=device(way), device_id_type=MESH)

        peers = peers + has(way).astype(jnp.int32)

    @pl.loop(0, steps)
    def _(n):
        for c in range(6):
            for x in range(tile_x):
                weighted[n, c, x] = zero

    for load in loads:
        load.wait()
    pl.semaphore_wait(barrier, peers)

    def part(d, low, high):
        return low if d < 0 else high

    def mat_copy(way):
        dx, dy = WAYS[way]
        if dx:
            src = mat.at[pl.ds(part(dx, 2, tile_x), 2)]
            dst = mat.at[pl.ds(part(dx, tile_x + 2, 0), 2)]
        else:
            at_row = pl.ds(part(dy, 0, rows - 2), 2)
            src, dst = mat.at[pl.ds(2, tile_x), at_row], mat_y.at[:, at_row]
        return pltpu.make_async_remote_copy(
            src_ref=src,
            dst_ref=dst,
            send_sem=m_send.at[way],
            recv_sem=m_recv.at[way],
            device_id=device(way),
            device_id_type=MESH,
        )

    def stress_copy(way, r):
        dx, dy = WAYS[way]
        if dx:
            src = stress.at[r, pl.ds(XY, 3), pl.ds(part(dx, 2, tile_x), 2)]
            dst = stress.at[r, pl.ds(XY, 3), pl.ds(part(dx, tile_x + 2, 0), 2)]
        else:
            at_row = pl.ds(part(dy, 0, rows - 2), 2)
            src = stress.at[r, pl.ds(0, 3), pl.ds(2, tile_x), at_row]
            dst = stress_y.at[r, :, :, at_row]
        return pltpu.make_async_remote_copy(
            src_ref=src,
            dst_ref=dst,
            send_sem=i_send.at[way, r],
            recv_sem=i_recv.at[way, r],
            device_id=device(way),
            device_id_type=MESH,
        )

    def vel_copy(way, p, r):
        dx, dy = WAYS[way]
        if dx and dy:
            src, dst = cor_out.at[p, r, way - 4], cor_in.at[p, r, way - 4]
        elif way >= 8:
            src = far_out.at[p, r, way - 8]
            dst = far_in.at[p, r, way - 8]
        elif dx:
            src = vel.at[p, r, :, pl.ds(part(dx, 4, tile_x + 2), 2)]
            dst = vel.at[p, r, :, pl.ds(part(dx, tile_x + 4, 2), 2)]
        else:
            at_row = pl.ds(part(dy, 0, rows - 4), 4)
            src = vel.at[p, r, :, pl.ds(4, tile_x), at_row]
            dst = vel_y.at[p, r, :, pl.ds(2, tile_x), at_row]
        return pltpu.make_async_remote_copy(
            src_ref=src,
            dst_ref=dst,
            send_sem=h_send.at[p, way, r],
            recv_sem=h_recv.at[p, way, r],
            device_id=device(way),
            device_id_type=MESH,
        )

    def send(copy, ways, *at):
        for way in ways:

            @pl.when(has(way))
            def _(way=way):
                copy(way, *at).start()

    def arrive(copy, ways, *at):
        for way in ways:

            @pl.when(has(BACK[way]))
            def _(way=way):
                copy(way, *at).wait_recv()

            @pl.when(has(way))
            def _(way=way):
                copy(way, *at).wait_send()

    corners = range(4, 8)
    sides, outer, all_ways = range(4), (8, 9, 4, 5, 6, 7), (4, 5, 6, 7, 0, 1, 2, 3, 8, 9)

    @pl.loop(0, recs)
    def _(r):
        send(stress_copy, sides, r)

    send(mat_copy, sides)

    def row_copy(d):
        to = (sx + d) % n_col
        return pltpu.make_async_remote_copy(
            src_ref=src_hbm.at[0, :, :, pl.ds(2 * to, 2)],
            dst_ref=rows_in.at[sx],
            send_sem=a_send.at[d - 1],
            recv_sem=a_recv.at[d - 1],
            device_id={"sta": 2 * to + sy},
            device_id_type=MESH,
        )

    for d in range(1, n_col):
        row_copy(d).start()

    def piece(q):
        return pltpu.make_async_remote_copy(
            src_ref=mine.at[q],
            dst_ref=other.at[q],
            send_sem=b_send.at[q],
            recv_sem=b_recv.at[q],
            device_id={"sta": 2 * sx + 1 - sy},
            device_id_type=MESH,
        )

    chunk = 4

    def ring(k, t):
        step = 1 if k % 2 == 0 else n_col - 1
        to = (sx + step) % n_col
        slot = sx if k < 2 else (sx + n_col - step) % n_col
        half = chunk // 2
        begin, size = (0, chunk) if k < 2 else ((k - 2) * half, half)
        ref = gath.at[slot, pl.ds(t * chunk + begin, size)]
        return pltpu.make_async_remote_copy(
            src_ref=ref,
            dst_ref=ref,
            send_sem=g_send.at[k, t],
            recv_sem=g_recv.at[k, t],
            device_id={"sta": 2 * to + sy},
            device_id_type=MESH,
        )

    def take_rows():
        own_rows.wait()
        for d in range(1, n_col):
            row_copy(d).wait()

    def pick_piece(q):
        m = q % steps
        p = pick_ref[q // steps, m]
        keep = p % 2 == sy
        for c in range(6):
            for j in range(2):
                v = rows_in[p // 2, m, c, j]
                mine[q, c, j] = jnp.where(keep, v, jnp.zeros_like(v))
        piece(q).start()

    def gather_rows(t):
        @pl.loop(t * chunk, (t + 1) * chunk)
        def _(q):
            piece(q).wait()
            for c in range(6):
                for j in range(2):
                    gath[sx, q, c, j] = mine[q, c, j] + other[q, c, j]

        ring(0, t).start()
        ring(1, t).start()

    def relay_rows(t):
        for k in range(4):
            if k < 2:
                ring(k, t).wait()
            else:
                ring(k, t).start()

    row_at = lax.broadcasted_iota(jnp.int32, (rows, depth), 0)
    lane_at = lax.broadcasted_iota(jnp.int32, (rows, depth), 1)
    first1, first2 = row_at < 1, row_at < 2
    last1, last2 = row_at >= rows - 1, row_at >= rows - 2
    src_at = lax.broadcasted_iota(jnp.int32, (2 * depth, depth), 0) % depth
    off = src_at - lax.broadcasted_iota(jnp.int32, (2 * depth, depth), 1)
    band = jnp.where(off == 1, 1.0, 0.0) - jnp.where(off == -1, 1.0, 0.0)
    band = band + 0.125 * (jnp.where(off == -2, 1.0, 0.0) - jnp.where(off == 2, 1.0, 0.0))
    band = band.astype(BF16)

    def diff_x(get, c, x):
        return (get(c, x + 1) - get(c, x - 1)) - 0.125 * (get(c, x + 2) - get(c, x - 2))

    def diff_y(t, e):
        up1 = pltpu.roll(jnp.where(first1, e, t), rows - 1, 0)
        up2 = pltpu.roll(jnp.where(first2, e, t), rows - 2, 0)
        dn1 = pltpu.roll(jnp.where(last1, e, t), 1, 0)
        dn2 = pltpu.roll(jnp.where(last2, e, t), 2, 0)
        return (up1 - dn1) - 0.125 * (up2 - dn2)

    def diff_z(f):
        planes = f.shape[0]
        f = f.reshape(planes * rows, depth)
        hi = f.astype(BF16)
        lo = (f - hi.astype(F32)).astype(BF16)
        both = jnp.concatenate([hi, lo], 1)
        d = jnp.dot(both, band, preferred_element_type=F32)
        return d.reshape(planes, rows, depth)

    tile = range(tile_x)

    def tables():
        def look(m, k):
            v = jnp.zeros((rows, depth), F32)
            for j in range(table_ref.shape[1]):
                v = jnp.where(m == j, table_ref[k, j], v)
            return v

        unit = TIME_STEP * STIFFNESS * C_NEAR
        for x in range(tile_x + 4):
            for k in (1, 2):
                coef[k, x] = unit * look(mat[x], k)
        for x in tile:
            for k in (1, 2):
                coef_y[k - 1, x] = unit * look(mat_y[x], k)

    def buoyancy():
        for x in tile:
            m = mat[x + 2]
            v = jnp.ones((rows, depth), F32)
            for j in range(table_ref.shape[1]):
                v = jnp.where(m == j, table_ref[0, j], v)
            coef[0, x + 2] = TIME_STEP * C_NEAR / v

    def velocity(n, p, r):
        def s(c, x):
            return stress[r, c, x + 2]

        def e(c, x):
            return stress_y[r, c, x]

        zx, zy, zz = (diff_z(stress[r, c, pl.ds(2, tile_x)]) for c in (XZ, YZ, ZZ))
        cell = cell_ref[0, r]
        cx = cell // (n_gy * rows) - gx * tile_x
        cy = cell % (n_gy * rows) - gy * rows
        amp = (AMPLITUDE / C_NEAR) * res_ref[0, r, n]
        spot = jnp.where((row_at == cy) & (lane_at == 0), amp, 0.0)
        for x in tile:
            b = coef[0, x + 2]
            fx = diff_x(s, XX, x) + diff_y(s(XY, x), e(XY, x)) + zx[x]
            fy = diff_x(s, XY, x) + diff_y(s(YY, x), e(YY, x)) + zy[x]
            fz = diff_x(s, XZ, x) + diff_y(s(YZ, x), e(YZ, x)) + zz[x]
            fz = fz + spot * jnp.where(cx == x, 1.0, 0.0)
            for c, f in ((VX, fx), (VY, fy), (VZ, fz)):
                vel[p, r, c, x + 4] = vel[1 - p, r, c, x + 4] + b * f
        for c in range(3):
            for side, (first, way) in enumerate(((6, 1), (tile_x + 1, -1))):
                for k in range(FAR):
                    far_out[p, r, side, c, k] = vel[p, r, c, first + way * k].astype(BF16)

        for way in corners:
            dx, dy = WAYS[way]
            got = None
            for k in range(4):
                f = vel[p, r, k // 2, part(dx, 4, tile_x + 2) + k % 2]
                shift = (2 * k + part(dy, 0, 2)) % rows
                f = pltpu.roll(f, shift, 0) if shift else f
                got = f if got is None else jnp.where(row_at >= 2 * k, f, got)
            cor_out[p, r, way - 4] = got.astype(BF16)

    def unpack(p, r):
        for low, high, first in ((6, 7, 0), (4, 5, tile_x + 2)):
            a, b = cor_in[p, r, low - 4].astype(F32), cor_in[p, r, high - 4].astype(F32)
            for k in range(4):
                fa = pltpu.roll(a, rows - 2 * k, 0) if k else a
                fb = pltpu.roll(b, rows - 2 - 2 * k, 0) if k < 3 else b
                vel_y[p, r, k // 2, first + k % 2] = jnp.where(row_at < 2, fa, fb)
        for c in range(3):
            for side, (first, way) in enumerate(((tile_x + 6, 1), (1, -1))):
                for k in range(FAR):
                    vel[p, r, c, first + way * k] = far_in[p, r, side, c, k].astype(F32)

    def strain(n, p, r, res, last):
        def v(c, x):
            return vel[p, r, c, x + 4]

        def e(c, x):
            return vel_y[p, r, c, x + 2]

        zx, zy, zz = (diff_z(vel[p, r, c, pl.ds(4, tile_x)]) for c in (VX, VY, VZ))
        for x in tile:
            la, mu = coef[1, x + 2], coef[2, x + 2]
            mu2 = mu + mu
            rxx = diff_x(v, VX, x)
            ryy = diff_y(v(VY, x), e(VY, x))
            rzz = zz[x]
            rxy = diff_y(v(VX, x), e(VX, x)) + diff_x(v, VY, x)
            rxz = zx[x] + diff_x(v, VZ, x)
            ryz = zy[x] + diff_y(v(VZ, x), e(VZ, x))
            tr = la * (rxx + ryy + rzz)
            put = ((XX, rxx), (YY, ryy), (ZZ, rzz), (XY, rxy), (XZ, rxz), (YZ, ryz))
            for k, (c, d) in enumerate(put):
                if last:
                    weighted[n, k, x] = d
                    continue
                weighted[n, k, x] = weighted[n, k, x] + res * d
                step = tr + mu2 * d if k < 3 else mu * d
                stress[r, c, x + 2] = stress[r, c, x + 2] + step

    def strain_edges(p, r):
        def v(c, x):
            return vel[p, r, c, x + 4]

        def e(c, x):
            return vel_y[p, r, c, x + 2]

        for low in (-2, tile_x):
            zx, zz = (diff_z(vel[p, r, c, pl.ds(low + 4, 2)]) for c in (VX, VZ))
            for k in range(2):
                x = low + k
                la, mu = coef[1, x + 2], coef[2, x + 2]
                rxx = diff_x(v, VX, x)
                ryy = diff_y(v(VY, x), e(VY, x))
                rxy = diff_y(v(VX, x), e(VX, x)) + diff_x(v, VY, x)
                rxz = zx[k] + diff_x(v, VZ, x)
                sxx = la * (rxx + ryy + zz[k]) + (mu + mu) * rxx
                for c, step in ((XX, sxx), (XY, mu * rxy), (XZ, mu * rxz)):
                    stress[r, c, x + 2] = stress[r, c, x + 2] + step
        zy, zz = (diff_z(vel_y[p, r, c, pl.ds(2, tile_x)]) for c in (VY, VZ))
        for x in tile:
            la, mu = coef_y[0, x], coef_y[1, x]
            rxx = diff_x(e, VX, x)
            ryy = diff_y(e(VY, x), v(VY, x))
            rxy = diff_y(e(VX, x), v(VX, x)) + diff_x(e, VY, x)
            ryz = zy[x] + diff_y(e(VZ, x), v(VZ, x))
            syy = la * (rxx + ryy + zz[x]) + (mu + mu) * ryy
            for c, step in ((YY, syy), (XY, mu * rxy), (YZ, mu * ryz)):
                stress_y[r, c, x] = stress_y[r, c, x] + step

    buoyancy()
    chunks = turns * steps // chunk

    @pl.loop(0, recs)
    def _(r):
        arrive(stress_copy, sides, r)
        velocity(0, 0, r)
        send(vel_copy, all_ways, 0, r)

    arrive(mat_copy, sides)
    tables()

    @pl.loop(0, steps - 1)
    def _(n):
        p = n % 2

        @pl.loop(0, recs)
        def _(r):
            arrive(vel_copy, sides, p, r)
            strain(n, p, r, res_ref[0, r, n], False)
            arrive(vel_copy, outer, p, r)
            unpack(p, r)
            strain_edges(p, r)
            velocity(n + 1, 1 - p, r)

            @pl.when(n < steps - 2)
            def _():
                send(vel_copy, all_ways, 1 - p, r)

            for t in range(chunks):
                pl.when((n == t + 2) & (r == 1))(functools.partial(gather_rows, t))

        pl.when(n == 0)(take_rows)

        @pl.when(n < chunks)
        def _():
            for j in range(chunk):
                pick_piece(n * chunk + j)

        for t in range(chunks - 1):
            pl.when(n == t + 3)(functools.partial(relay_rows, t))

    end = (steps - 1) % 2
    for c in range(3):
        for x in tile:
            total = res_ref[0, 0, steps - 1] * vel[end, 0, c, x + 4]
            for r in range(1, recs):
                total = total + res_ref[0, r, steps - 1] * vel[end, r, c, x + 4]
            vel[end, 0, c, x + 4] = total
    send(vel_copy, sides, end, 0)
    relay_rows(chunks - 1)

    for x in range(tile_x):
        for k in range(2):
            acc[x, k] = zero

    scale = KERNEL_SCALE * C_NEAR

    def correlate(n):
        share = [listed_ref[t, n, sta].astype(F32) for t in range(turns)]
        for x in range(tile_x):
            comb = []
            for c in range(6):
                total = None
                for t in range(turns):
                    v = share[t] * gath[x // 2, t * steps + n, c, x % 2].astype(F32)
                    total = v if total is None else total + v
                comb.append(total)
            w = [weighted[n, k, x] for k in range(6)]
            lam = (comb[0] + comb[1] + comb[2]) * (w[0] + w[1] + w[2])
            mu = comb[0] * w[0]
            for c in range(1, 6):
                mu = mu + comb[c] * w[c]
            acc[x, 0] = acc[x, 0] + scale * lam
            acc[x, 1] = acc[x, 1] + (2.0 * scale) * mu

    def landed(t):
        ring(2, t).wait()
        ring(3, t).wait()

    early = steps // 2
    for t in range(chunks - 1):
        landed(t)
    pl.loop(0, early)(correlate)
    arrive(vel_copy, sides, end, 0)
    strain(steps - 1, end, 0, None, True)
    landed(chunks - 1)
    pl.loop(early, steps)(correlate)

    def share_copy(d):
        to = (sta + d) % n_sta
        return pltpu.make_async_remote_copy(
            src_ref=acc.at[to],
            dst_ref=parts.at[d],
            send_sem=r_send.at[d],
            recv_sem=r_recv.at[d],
            device_id={"sta": to},
            device_id_type=MESH,
        )

    for d in range(1, n_sta):
        share_copy(d).start()
    for k in range(2):
        out_ref[k, 0] = acc[sta, k]
    for d in range(1, n_sta):
        share_copy(d).wait()
        for k in range(2):
            out_ref[k, 0] = out_ref[k, 0] + parts[d, k]


def local(rec_state, source_strain, material, material_table, residual, rec_cell, listed, src_pick):
    _, recs, _, tile_x, tile_y, depth = rec_state.shape
    steps = source_strain.shape[1]
    turns = listed.shape[0]
    n_sta = lax.axis_size("sta")
    n_col = n_sta // 2
    plane = (tile_y, depth)
    hbm = pl.BlockSpec(memory_space=pltpu.HBM)
    table = material_table.T
    smalls = (table, residual, rec_cell, listed, src_pick)
    dma = pltpu.SemaphoreType.DMA
    return pl.pallas_call(
        body,
        out_shape=jax.ShapeDtypeStruct((2, 1, *plane), F32),
        in_specs=[hbm] * 8,
        out_specs=pl.BlockSpec(memory_space=pltpu.VMEM),
        scratch_shapes=[
            pltpu.VMEM((recs, 6, tile_x + 4, *plane), F32),
            pltpu.VMEM((recs, 3, tile_x, *plane), F32),
            pltpu.VMEM((2, recs, 3, tile_x + 8, *plane), F32),
            pltpu.VMEM((2, recs, 3, tile_x + 4, *plane), F32),
            pltpu.VMEM((2, recs, 2, 3, FAR, *plane), BF16),
            pltpu.VMEM((2, recs, 2, 3, FAR, *plane), BF16),
            pltpu.VMEM((2, recs, 4, *plane), BF16),
            pltpu.VMEM((2, recs, 4, *plane), BF16),
            pltpu.VMEM((steps, 6, tile_x, *plane), F32),
            pltpu.VMEM((tile_x + 4, *plane), jnp.int32),
            pltpu.VMEM((tile_x, *plane), jnp.int32),
            pltpu.VMEM((3, tile_x + 4, *plane), F32),
            pltpu.VMEM((2, tile_x, *plane), F32),
            pltpu.VMEM((n_col, steps, 6, 2, *plane), BF16),
            pltpu.VMEM((turns * steps, 6, 2, *plane), BF16),
            pltpu.VMEM((turns * steps, 6, 2, *plane), BF16),
            pltpu.VMEM((n_col, turns * steps, 6, 2, *plane), BF16),
            pltpu.VMEM((tile_x, 2, *plane), F32),
            pltpu.VMEM((n_sta, 2, *plane), F32),
            *[pltpu.SMEM(a.shape, a.dtype) for a in smalls],
            dma((16,)),
            dma((4,)),
            dma((4,)),
            dma((4, recs)),
            dma((4, recs)),
            dma((2, 10, recs)),
            dma((2, 10, recs)),
            dma((n_col - 1,)),
            dma((n_col - 1,)),
            dma((turns * steps,)),
            dma((turns * steps,)),
            dma((4, turns * steps // 4)),
            dma((4, turns * steps // 4)),
            dma((n_sta,)),
            dma((n_sta,)),
        ],
        compiler_params=pltpu.CompilerParams(
            collective_id=0, has_side_effects=True
        ),
        name="kernels",
    )(rec_state, source_strain, material, *smalls)


def solution(mesh):
    in_specs = (
        P("sta", None, None, "gx", "gy", None),
        P("sta", None, None, "gx", "gy", None),
        P("gx", "gy", None),
        P(),
        P("sta", None, None),
        P("sta", None),
        P(),
        P(),
    )
    out_specs = P(None, ("gx", "sta"), "gy", None)
    return jax.shard_map(local, mesh=mesh, in_specs=in_specs, out_specs=out_specs, check_vma=False)
```

```python
import functools

import jax
import jax.numpy as jnp
from jax import lax
from jax.experimental import pallas as pl
from jax.experimental.pallas import tpu as pltpu
from jax.sharding import PartitionSpec as P

MESH = pl.DeviceIdType.MESH
F32 = jnp.float32
BF16 = jnp.bfloat16

C_NEAR = 8.0 / 12.0
TIME_STEP = 0.25
AMPLITUDE = 4.0
KERNEL_SCALE = 0.0625
STIFFNESS = 0.3

YY, YZ, XY, XX, XZ, ZZ = range(6)
STRESS_FROM = (1, 5, 3, 0, 4, 2)
VX, VY, VZ = range(3)
WAYS = ((-1, 0), (1, 0), (0, -1), (0, 1), (-1, -1), (-1, 1), (1, -1), (1, 1), (-1, 0), (1, 0))
BACK = (1, 0, 3, 2, 7, 6, 5, 4, 9, 8)
FAR = 2


def body(
    rec_hbm,
    src_hbm,
    mat_hbm,
    table_hbm,
    res_hbm,
    cell_hbm,
    listed_hbm,
    pick_hbm,
    out_ref,
    stress,
    stress_y,
    vel,
    vel_y,
    far_out,
    far_in,
    cor_out,
    cor_in,
    weighted,
    mat,
    mat_y,
    coef,
    coef_y,
    rows_in,
    mine,
    other,
    gath,
    acc,
    parts,
    table_ref,
    res_ref,
    cell_ref,
    listed_ref,
    pick_ref,
    in_sem,
    m_send,
    m_recv,
    i_send,
    i_recv,
    h_send,
    h_recv,
    a_send,
    a_recv,
    b_send,
    b_recv,
    g_send,
    g_recv,
    r_send,
    r_recv,
):
    recs = stress.shape[0]
    steps = weighted.shape[0]
    tile_x, rows, depth = coef_y.shape[1:]
    turns = listed_ref.shape[0]
    n_sta = parts.shape[0]
    n_col = gath.shape[0]
    gx, gy, sta = lax.axis_index("gx"), lax.axis_index("gy"), lax.axis_index("sta")
    n_gx, n_gy = lax.axis_size("gx"), lax.axis_size("gy")
    sx, sy = sta // 2, sta % 2

    loads = [pltpu.make_async_copy(mat_hbm, mat.at[pl.ds(2, tile_x)], in_sem.at[0])]
    for c, src in enumerate(STRESS_FROM):
        loads.append(
            pltpu.make_async_copy(
                rec_hbm.at[0, :, 3 + src], stress.at[:, c, pl.ds(2, tile_x)], in_sem.at[1 + c]
            )
        )
    for c in range(3):
        loads.append(
            pltpu.make_async_copy(
                rec_hbm.at[0, :, c], vel.at[1, :, c, pl.ds(4, tile_x)], in_sem.at[7 + c]
            )
        )
    own_rows = pltpu.make_async_copy(
        src_hbm.at[0, :, :, pl.ds(2 * sx, 2)], rows_in.at[sx], in_sem.at[10]
    )
    smalls = (
        (table_hbm, table_ref),
        (res_hbm, res_ref),
        (cell_hbm, cell_ref),
        (listed_hbm, listed_ref),
        (pick_hbm, pick_ref),
    )
    for k, (a, b) in enumerate(smalls):
        loads.insert(1 + k, pltpu.make_async_copy(a, b, in_sem.at[11 + k]))
    for load in loads:
        load.start()
    own_rows.start()

    zero = jnp.zeros((rows, depth), F32)
    none = jnp.full((rows, depth), -1, jnp.int32)
    for row in (0, 1, tile_x + 2, tile_x + 3):
        mat[row] = none
    for row in range(tile_x):
        mat_y[row] = none

    @pl.loop(0, recs)
    def _(r):
        for p in range(2):
            for k in range(4):
                cor_in[p, r, k] = zero.astype(BF16)
        for c in range(6):
            for row in (0, 1, tile_x + 2, tile_x + 3):
                stress[r, c, row] = zero
        for c in range(3):
            for row in range(tile_x):
                stress_y[r, c, row] = zero
            for p in range(2):
                for row in range(4):
                    vel[p, r, c, row] = zero
                    vel[p, r, c, tile_x + 4 + row] = zero
                for row in range(tile_x + 4):
                    vel_y[p, r, c, row] = zero
                for side in range(2):
                    for k in range(FAR):
                        far_in[p, r, side, c, k] = zero.astype(BF16)

    barrier = pltpu.get_barrier_semaphore()

    def has(way):
        dx, dy = WAYS[way]
        ok = None
        for d, at, count in ((dx, gx, n_gx), (dy, gy, n_gy)):
            if d:
                one = at > 0 if d < 0 else at < count - 1
                ok = one if ok is None else ok & one
        return ok

    def device(way):
        dx, dy = WAYS[way]
        return {"gx": jnp.clip(gx + dx, 0, n_gx - 1), "gy": jnp.clip(gy + dy, 0, n_gy - 1)}

    column = [2 * ((sx + d) % n_col) + sy for d in range(1, n_col)] + [2 * sx + 1 - sy]
    for to in column:
        pl.semaphore_signal(barrier, inc=1, device_id={"sta": to}, device_id_type=MESH)
    peers = len(column)
    for way in range(8):

        @pl.when(has(way))
        def _(way=way):
            pl.semaphore_signal(barrier, inc=1, device_id=device(way), device_id_type=MESH)

        peers = peers + has(way).astype(jnp.int32)

    @pl.loop(0, steps)
    def _(n):
        for c in range(6):
            for x in range(tile_x):
                weighted[n, c, x] = zero

    for load in loads:
        load.wait()
    pl.semaphore_wait(barrier, peers)

    def part(d, low, high):
        return low if d < 0 else high

    def mat_copy(way):
        dx, dy = WAYS[way]
        if dx:
            src = mat.at[pl.ds(part(dx, 2, tile_x), 2)]
            dst = mat.at[pl.ds(part(dx, tile_x + 2, 0), 2)]
        else:
            at_row = pl.ds(part(dy, 0, rows - 2), 2)
            src, dst = mat.at[pl.ds(2, tile_x), at_row], mat_y.at[:, at_row]
        return pltpu.make_async_remote_copy(
            src_ref=src,
            dst_ref=dst,
            send_sem=m_send.at[way],
            recv_sem=m_recv.at[way],
            device_id=device(way),
            device_id_type=MESH,
        )

    def stress_copy(way, r):
        dx, dy = WAYS[way]
        if dx:
            src = stress.at[r, pl.ds(XY, 3), pl.ds(part(dx, 2, tile_x), 2)]
            dst = stress.at[r, pl.ds(XY, 3), pl.ds(part(dx, tile_x + 2, 0), 2)]
        else:
            at_row = pl.ds(part(dy, 0, rows - 2), 2)
            src = stress.at[r, pl.ds(0, 3), pl.ds(2, tile_x), at_row]
            dst = stress_y.at[r, :, :, at_row]
        return pltpu.make_async_remote_copy(
            src_ref=src,
            dst_ref=dst,
            send_sem=i_send.at[way, r],
            recv_sem=i_recv.at[way, r],
            device_id=device(way),
            device_id_type=MESH,
        )

    def vel_copy(way, p, r):
        dx, dy = WAYS[way]
        if dx and dy:
            src, dst = cor_out.at[p, r, way - 4], cor_in.at[p, r, way - 4]
        elif way >= 8:
            src = far_out.at[p, r, way - 8]
            dst = far_in.at[p, r, way - 8]
        elif dx:
            src = vel.at[p, r, :, pl.ds(part(dx, 4, tile_x + 2), 2)]
            dst = vel.at[p, r, :, pl.ds(part(dx, tile_x + 4, 2), 2)]
        else:
            at_row = pl.ds(part(dy, 0, rows - 4), 4)
            src = vel.at[p, r, :, pl.ds(4, tile_x), at_row]
            dst = vel_y.at[p, r, :, pl.ds(2, tile_x), at_row]
        return pltpu.make_async_remote_copy(
            src_ref=src,
            dst_ref=dst,
            send_sem=h_send.at[p, way, r],
            recv_sem=h_recv.at[p, way, r],
            device_id=device(way),
            device_id_type=MESH,
        )

    def send(copy, ways, *at):
        for way in ways:

            @pl.when(has(way))
            def _(way=way):
                copy(way, *at).start()

    def arrive(copy, ways, *at):
        for way in ways:

            @pl.when(has(BACK[way]))
            def _(way=way):
                copy(way, *at).wait_recv()

            @pl.when(has(way))
            def _(way=way):
                copy(way, *at).wait_send()

    corners = range(4, 8)
    sides, outer, all_ways = range(4), (8, 9, 4, 5, 6, 7), (4, 5, 6, 7, 0, 1, 2, 3, 8, 9)

    @pl.loop(0, recs)
    def _(r):
        send(stress_copy, sides, r)

    send(mat_copy, sides)

    def row_copy(d):
        to = (sx + d) % n_col
        return pltpu.make_async_remote_copy(
            src_ref=src_hbm.at[0, :, :, pl.ds(2 * to, 2)],
            dst_ref=rows_in.at[sx],
            send_sem=a_send.at[d - 1],
            recv_sem=a_recv.at[d - 1],
            device_id={"sta": 2 * to + sy},
            device_id_type=MESH,
        )

    for d in range(1, n_col):
        row_copy(d).start()

    def piece(q):
        return pltpu.make_async_remote_copy(
            src_ref=mine.at[q],
            dst_ref=other.at[q],
            send_sem=b_send.at[q],
            recv_sem=b_recv.at[q],
            device_id={"sta": 2 * sx + 1 - sy},
            device_id_type=MESH,
        )

    chunk = 4

    def ring(k, t):
        step = 1 if k % 2 == 0 else n_col - 1
        to = (sx + step) % n_col
        slot = sx if k < 2 else (sx + n_col - step) % n_col
        half = chunk // 2
        begin, size = (0, chunk) if k < 2 else ((k - 2) * half, half)
        ref = gath.at[slot, pl.ds(t * chunk + begin, size)]
        return pltpu.make_async_remote_copy(
            src_ref=ref,
            dst_ref=ref,
            send_sem=g_send.at[k, t],
            recv_sem=g_recv.at[k, t],
            device_id={"sta": 2 * to + sy},
            device_id_type=MESH,
        )

    def take_rows():
        own_rows.wait()
        for d in range(1, n_col):
            row_copy(d).wait()

    def pick_piece(q):
        m = q % steps
        p = pick_ref[q // steps, m]
        keep = p % 2 == sy
        for c in range(6):
            for j in range(2):
                v = rows_in[p // 2, m, c, j]
                mine[q, c, j] = jnp.where(keep, v, jnp.zeros_like(v))
        piece(q).start()

    def gather_rows(t):
        @pl.loop(t * chunk, (t + 1) * chunk)
        def _(q):
            piece(q).wait()
            for c in range(6):
                for j in range(2):
                    gath[sx, q, c, j] = mine[q, c, j] + other[q, c, j]

        ring(0, t).start()
        ring(1, t).start()

    def relay_rows(t):
        for k in range(4):
            if k < 2:
                ring(k, t).wait()
            else:
                ring(k, t).start()

    row_at = lax.broadcasted_iota(jnp.int32, (rows, depth), 0)
    lane_at = lax.broadcasted_iota(jnp.int32, (rows, depth), 1)
    first1, first2 = row_at < 1, row_at < 2
    last1, last2 = row_at >= rows - 1, row_at >= rows - 2
    src_at = lax.broadcasted_iota(jnp.int32, (2 * depth, depth), 0) % depth
    off = src_at - lax.broadcasted_iota(jnp.int32, (2 * depth, depth), 1)
    band = jnp.where(off == 1, 1.0, 0.0) - jnp.where(off == -1, 1.0, 0.0)
    band = band + 0.125 * (jnp.where(off == -2, 1.0, 0.0) - jnp.where(off == 2, 1.0, 0.0))
    band = band.astype(BF16)

    def diff_x(get, c, x):
        return (get(c, x + 1) - get(c, x - 1)) - 0.125 * (get(c, x + 2) - get(c, x - 2))

    def diff_y(t, e):
        up1 = pltpu.roll(jnp.where(first1, e, t), rows - 1, 0)
        up2 = pltpu.roll(jnp.where(first2, e, t), rows - 2, 0)
        dn1 = pltpu.roll(jnp.where(last1, e, t), 1, 0)
        dn2 = pltpu.roll(jnp.where(last2, e, t), 2, 0)
        return (up1 - dn1) - 0.125 * (up2 - dn2)

    def diff_z(f):
        planes = f.shape[0]
        f = f.reshape(planes * rows, depth)
        hi = f.astype(BF16)
        lo = (f - hi.astype(F32)).astype(BF16)
        both = jnp.concatenate([hi, lo], 1)
        d = jnp.dot(both, band, preferred_element_type=F32)
        return d.reshape(planes, rows, depth)

    tile = range(tile_x)

    def tables():
        def look(m, k):
            v = jnp.zeros((rows, depth), F32)
            for j in range(table_ref.shape[1]):
                v = jnp.where(m == j, table_ref[k, j], v)
            return v

        unit = TIME_STEP * STIFFNESS * C_NEAR
        for x in range(tile_x + 4):
            for k in (1, 2):
                coef[k, x] = unit * look(mat[x], k)
        for x in tile:
            for k in (1, 2):
                coef_y[k - 1, x] = unit * look(mat_y[x], k)

    def buoyancy():
        for x in tile:
            m = mat[x + 2]
            v = jnp.ones((rows, depth), F32)
            for j in range(table_ref.shape[1]):
                v = jnp.where(m == j, table_ref[0, j], v)
            coef[0, x + 2] = TIME_STEP * C_NEAR / v

    def velocity(n, p, r):
        def s(c, x):
            return stress[r, c, x + 2]

        def e(c, x):
            return stress_y[r, c, x]

        zx, zy, zz = (diff_z(stress[r, c, pl.ds(2, tile_x)]) for c in (XZ, YZ, ZZ))
        cell = cell_ref[0, r]
        cx = cell // (n_gy * rows) - gx * tile_x
        cy = cell % (n_gy * rows) - gy * rows
        amp = (AMPLITUDE / C_NEAR) * res_ref[0, r, n]
        spot = jnp.where((row_at == cy) & (lane_at == 0), amp, 0.0)
        for x in tile:
            b = coef[0, x + 2]
            fx = diff_x(s, XX, x) + diff_y(s(XY, x), e(XY, x)) + zx[x]
            fy = diff_x(s, XY, x) + diff_y(s(YY, x), e(YY, x)) + zy[x]
            fz = diff_x(s, XZ, x) + diff_y(s(YZ, x), e(YZ, x)) + zz[x]
            fz = fz + spot * jnp.where(cx == x, 1.0, 0.0)
            for c, f in ((VX, fx), (VY, fy), (VZ, fz)):
                vel[p, r, c, x + 4] = vel[1 - p, r, c, x + 4] + b * f
        for c in range(3):
            for side, (first, way) in enumerate(((6, 1), (tile_x + 1, -1))):
                for k in range(FAR):
                    far_out[p, r, side, c, k] = vel[p, r, c, first + way * k].astype(BF16)

        for way in corners:
            dx, dy = WAYS[way]
            got = None
            for k in range(4):
                f = vel[p, r, k // 2, part(dx, 4, tile_x + 2) + k % 2]
                shift = (2 * k + part(dy, 0, 2)) % rows
                f = pltpu.roll(f, shift, 0) if shift else f
                got = f if got is None else jnp.where(row_at >= 2 * k, f, got)
            cor_out[p, r, way - 4] = got.astype(BF16)

    def unpack(p, r):
        for low, high, first in ((6, 7, 0), (4, 5, tile_x + 2)):
            a, b = cor_in[p, r, low - 4].astype(F32), cor_in[p, r, high - 4].astype(F32)
            for k in range(4):
                fa = pltpu.roll(a, rows - 2 * k, 0) if k else a
                fb = pltpu.roll(b, rows - 2 - 2 * k, 0) if k < 3 else b
                vel_y[p, r, k // 2, first + k % 2] = jnp.where(row_at < 2, fa, fb)
        for c in range(3):
            for side, (first, way) in enumerate(((tile_x + 6, 1), (1, -1))):
                for k in range(FAR):
                    vel[p, r, c, first + way * k] = far_in[p, r, side, c, k].astype(F32)

    def strain(n, p, r, res, last):
        def v(c, x):
            return vel[p, r, c, x + 4]

        def e(c, x):
            return vel_y[p, r, c, x + 2]

        zx, zy, zz = (diff_z(vel[p, r, c, pl.ds(4, tile_x)]) for c in (VX, VY, VZ))
        for x in tile:
            la, mu = coef[1, x + 2], coef[2, x + 2]
            mu2 = mu + mu
            rxx = diff_x(v, VX, x)
            ryy = diff_y(v(VY, x), e(VY, x))
            rzz = zz[x]
            rxy = diff_y(v(VX, x), e(VX, x)) + diff_x(v, VY, x)
            rxz = zx[x] + diff_x(v, VZ, x)
            ryz = zy[x] + diff_y(v(VZ, x), e(VZ, x))
            tr = la * (rxx + ryy + rzz)
            put = ((XX, rxx), (YY, ryy), (ZZ, rzz), (XY, rxy), (XZ, rxz), (YZ, ryz))
            for k, (c, d) in enumerate(put):
                if last:
                    weighted[n, k, x] = d
                    continue
                weighted[n, k, x] = weighted[n, k, x] + res * d
                step = tr + mu2 * d if k < 3 else mu * d
                stress[r, c, x + 2] = stress[r, c, x + 2] + step

    def strain_edges(p, r):
        def v(c, x):
            return vel[p, r, c, x + 4]

        def e(c, x):
            return vel_y[p, r, c, x + 2]

        for low in (-2, tile_x):
            zx, zz = (diff_z(vel[p, r, c, pl.ds(low + 4, 2)]) for c in (VX, VZ))
            for k in range(2):
                x = low + k
                la, mu = coef[1, x + 2], coef[2, x + 2]
                rxx = diff_x(v, VX, x)
                ryy = diff_y(v(VY, x), e(VY, x))
                rxy = diff_y(v(VX, x), e(VX, x)) + diff_x(v, VY, x)
                rxz = zx[k] + diff_x(v, VZ, x)
                sxx = la * (rxx + ryy + zz[k]) + (mu + mu) * rxx
                for c, step in ((XX, sxx), (XY, mu * rxy), (XZ, mu * rxz)):
                    stress[r, c, x + 2] = stress[r, c, x + 2] + step
        zy, zz = (diff_z(vel_y[p, r, c, pl.ds(2, tile_x)]) for c in (VY, VZ))
        for x in tile:
            la, mu = coef_y[0, x], coef_y[1, x]
            rxx = diff_x(e, VX, x)
            ryy = diff_y(e(VY, x), v(VY, x))
            rxy = diff_y(e(VX, x), v(VX, x)) + diff_x(e, VY, x)
            ryz = zy[x] + diff_y(e(VZ, x), v(VZ, x))
            syy = la * (rxx + ryy + zz[x]) + (mu + mu) * ryy
            for c, step in ((YY, syy), (XY, mu * rxy), (YZ, mu * ryz)):
                stress_y[r, c, x] = stress_y[r, c, x] + step

    buoyancy()
    chunks = turns * steps // chunk

    @pl.loop(0, recs)
    def _(r):
        arrive(stress_copy, sides, r)
        velocity(0, 0, r)
        send(vel_copy, all_ways, 0, r)

    arrive(mat_copy, sides)
    tables()

    @pl.loop(0, steps - 1)
    def _(n):
        p = n % 2

        @pl.loop(0, recs)
        def _(r):
            arrive(vel_copy, sides, p, r)
            strain(n, p, r, res_ref[0, r, n], False)
            arrive(vel_copy, outer, p, r)
            unpack(p, r)
            strain_edges(p, r)
            velocity(n + 1, 1 - p, r)

            @pl.when(n < steps - 2)
            def _():
                send(vel_copy, all_ways, 1 - p, r)

            for t in range(chunks):
                pl.when((n == t + 2) & (r == 1))(functools.partial(gather_rows, t))

        pl.when(n == 0)(take_rows)

        @pl.when(n < chunks)
        def _():
            for j in range(chunk):
                pick_piece(n * chunk + j)

        for t in range(chunks - 1):
            pl.when(n == t + 3)(functools.partial(relay_rows, t))

    end = (steps - 1) % 2
    for c in range(3):
        for x in tile:
            total = res_ref[0, 0, steps - 1] * vel[end, 0, c, x + 4]
            for r in range(1, recs):
                total = total + res_ref[0, r, steps - 1] * vel[end, r, c, x + 4]
            vel[end, 0, c, x + 4] = total
    send(vel_copy, sides, end, 0)
    relay_rows(chunks - 1)

    for x in range(tile_x):
        for k in range(2):
            acc[x, k] = zero

    scale = KERNEL_SCALE * C_NEAR

    def correlate(n):
        share = [listed_ref[t, n, sta].astype(F32) for t in range(turns)]
        for x in range(tile_x):
            comb = []
            for c in range(6):
                total = None
                for t in range(turns):
                    v = share[t] * gath[x // 2, t * steps + n, c, x % 2].astype(F32)
                    total = v if total is None else total + v
                comb.append(total)
            w = [weighted[n, k, x] for k in range(6)]
            lam = (comb[0] + comb[1] + comb[2]) * (w[0] + w[1] + w[2])
            mu = comb[0] * w[0]
            for c in range(1, 6):
                mu = mu + comb[c] * w[c]
            acc[x, 0] = acc[x, 0] + scale * lam
            acc[x, 1] = acc[x, 1] + (2.0 * scale) * mu

    def landed(t):
        ring(2, t).wait()
        ring(3, t).wait()

    early = steps // 2
    for t in range(chunks - 1):
        landed(t)
    pl.loop(0, early)(correlate)
    arrive(vel_copy, sides, end, 0)
    strain(steps - 1, end, 0, None, True)
    landed(chunks - 1)
    pl.loop(early, steps)(correlate)

    def share_copy(d):
        to = (sta + d) % n_sta
        return pltpu.make_async_remote_copy(
            src_ref=acc.at[to],
            dst_ref=parts.at[d],
            send_sem=r_send.at[d],
            recv_sem=r_recv.at[d],
            device_id={"sta": to},
            device_id_type=MESH,
        )

    far_first = sorted(range(1, n_sta), key=lambda d: abs(d - n_sta // 2))
    for d in far_first:
        share_copy(d).start()
    for k in range(2):
        out_ref[k, 0] = acc[sta, k]
    for d in reversed(far_first):
        share_copy(d).wait()
        for k in range(2):
            out_ref[k, 0] = out_ref[k, 0] + parts[d, k]


def local(rec_state, source_strain, material, material_table, residual, rec_cell, listed, src_pick):
    _, recs, _, tile_x, tile_y, depth = rec_state.shape
    steps = source_strain.shape[1]
    turns = listed.shape[0]
    n_sta = lax.axis_size("sta")
    n_col = n_sta // 2
    plane = (tile_y, depth)
    hbm = pl.BlockSpec(memory_space=pltpu.HBM)
    table = material_table.T
    smalls = (table, residual, rec_cell, listed, src_pick)
    dma = pltpu.SemaphoreType.DMA
    return pl.pallas_call(
        body,
        out_shape=jax.ShapeDtypeStruct((2, 1, *plane), F32),
        in_specs=[hbm] * 8,
        out_specs=pl.BlockSpec(memory_space=pltpu.VMEM),
        scratch_shapes=[
            pltpu.VMEM((recs, 6, tile_x + 4, *plane), F32),
            pltpu.VMEM((recs, 3, tile_x, *plane), F32),
            pltpu.VMEM((2, recs, 3, tile_x + 8, *plane), F32),
            pltpu.VMEM((2, recs, 3, tile_x + 4, *plane), F32),
            pltpu.VMEM((2, recs, 2, 3, FAR, *plane), BF16),
            pltpu.VMEM((2, recs, 2, 3, FAR, *plane), BF16),
            pltpu.VMEM((2, recs, 4, *plane), BF16),
            pltpu.VMEM((2, recs, 4, *plane), BF16),
            pltpu.VMEM((steps, 6, tile_x, *plane), F32),
            pltpu.VMEM((tile_x + 4, *plane), jnp.int32),
            pltpu.VMEM((tile_x, *plane), jnp.int32),
            pltpu.VMEM((3, tile_x + 4, *plane), F32),
            pltpu.VMEM((2, tile_x, *plane), F32),
            pltpu.VMEM((n_col, steps, 6, 2, *plane), BF16),
            pltpu.VMEM((turns * steps, 6, 2, *plane), BF16),
            pltpu.VMEM((turns * steps, 6, 2, *plane), BF16),
            pltpu.VMEM((n_col, turns * steps, 6, 2, *plane), BF16),
            pltpu.VMEM((tile_x, 2, *plane), F32),
            pltpu.VMEM((n_sta, 2, *plane), F32),
            *[pltpu.SMEM(a.shape, a.dtype) for a in smalls],
            dma((16,)),
            dma((4,)),
            dma((4,)),
            dma((4, recs)),
            dma((4, recs)),
            dma((2, 10, recs)),
            dma((2, 10, recs)),
            dma((n_col - 1,)),
            dma((n_col - 1,)),
            dma((turns * steps,)),
            dma((turns * steps,)),
            dma((4, turns * steps // 4)),
            dma((4, turns * steps // 4)),
            dma((n_sta,)),
            dma((n_sta,)),
        ],
        compiler_params=pltpu.CompilerParams(
            collective_id=0, has_side_effects=True
        ),
        name="kernels",
    )(rec_state, source_strain, material, *smalls)


def solution(mesh):
    in_specs = (
        P("sta", None, None, "gx", "gy", None),
        P("sta", None, None, "gx", "gy", None),
        P("gx", "gy", None),
        P(),
        P("sta", None, None),
        P("sta", None),
        P(),
        P(),
    )
    out_specs = P(None, ("gx", "sta"), "gy", None)
    return jax.shard_map(local, mesh=mesh, in_specs=in_specs, out_specs=out_specs, check_vma=False)
```
